512 devices in a mesh: ctx: 64 (over z, y), head: 8 (over x, core).
Axes of the slice: x: 4, y: 4, z: 16, core: 2. Of those that a mesh axis runs over, the one named last changes fastest.
Arguments:
- hidden_states: bfloat16 [8192, 8192], P('ctx'), may hold values from -16 to 16
- queries: bfloat16 [8192, 8192], P('ctx', 'head'), may hold values from -110 to 110
- keys: bfloat16 [8192, 1024], P('ctx', 'head'), may hold values from -6 to 6
- values: bfloat16 [8192, 1024], P('ctx', 'head'), may hold values from -6 to 6
- output_gradient: bfloat16 [8192, 8192], P('ctx', 'head'), may hold values from -12 to 12
- doc_blocks: int32 [5], replicated, may hold values from 1 to 24, 64 in all
Outputs:
- ascent_key: float32 [8192, 1024], P('ctx', 'head')
- ascent_value: float32 [8192, 1024], P('ctx', 'head')
The draws below stay inside these ranges and needn't reach their ends.
Inputs may be any that keep to these rules, and one draw needn't show every extreme that they name: `doc_blocks`: document lengths count blocks of 128 tokens; they sum to 64, and the longest holds exactly 24 blocks.
All inputs are finite; a program needn't handle non-finite values.
Results may differ from the reference program's by a relative error of at most 0.029.
Values may be sent and summed in bfloat16 or wider, within the bound.
No kernel may reach another device: no remote copies, remote signals or barrier semaphores. Data moves between devices by JAX's collectives and lax.ppermute only.
A program may use at most 64 MiB of HBM per device.

```python
import math
import jax
import jax.numpy as jnp
import numpy as np
from jax import lax

MODEL_WIDTH = 8192
QUERY_HEADS = 64
KEY_VALUE_HEADS = 8
HEAD_SIZE = 128
TOK_DEV = 128
BLOCK_TOKENS = 128
REACH = 24
DOCS = 5
PACKED_TOKENS = 8192


def draw_hidden_states(key, part):
    first, second = jax.random.split(jax.random.fold_in(key, 11), 2)
    trend = jnp.exp(0.55 * jnp.arange(MODEL_WIDTH, dtype=jnp.float32) / MODEL_WIDTH)
    rough = jnp.exp(1.15 * jax.random.uniform(second, (MODEL_WIDTH,), jnp.float32))
    base = jnp.clip(jax.random.normal(first, (PACKED_TOKENS, MODEL_WIDTH), jnp.float32), -6.0, 6.0)
    return (base * trend[None, :] * rough[None, :] * 0.45).astype(jnp.bfloat16)


def draw_queries(key, part):
    first = jax.random.fold_in(jax.random.fold_in(key, 23), 0)
    return jnp.clip(jax.random.normal(first, (PACKED_TOKENS, QUERY_HEADS * HEAD_SIZE), jnp.float32), -6.0, 6.0).astype(jnp.bfloat16)


def draw_output_gradient(key, part):
    first, second = jax.random.split(jax.random.fold_in(key, 37), 2)
    columns = jnp.exp(1.15 * jax.random.uniform(second, (QUERY_HEADS * HEAD_SIZE,), jnp.float32))
    base = jnp.clip(jax.random.normal(first, (PACKED_TOKENS, QUERY_HEADS * HEAD_SIZE), jnp.float32), -6.0, 6.0)
    return (base * columns[None, :] * 0.6).astype(jnp.bfloat16)


def block_scale(rng, extent, cuts, smallest, largest):
    factor_of, own = 1.0, jax.random.fold_in(rng, 6)
    for axis_at, parts in cuts:
        steps = jnp.exp(jax.random.uniform(jax.random.fold_in(own, axis_at), (parts,), jnp.float32, smallest / len(cuts), largest / len(cuts)))
        factor_of = factor_of * jnp.repeat(steps, extent[axis_at] // parts).reshape([-1 if axis == axis_at else 1 for axis in range(len(extent))])
    return factor_of


def split_up(amount, total, bound, skew):
    weights = [(1 << 20) // math.isqrt(standing ** skew) + 1 for standing in range(2, amount + 1)]
    surplus, counts = total - bound - (amount - 1), [1] * (amount - 1)
    while surplus > 0:
        candidates = [i for i in range(amount - 1) if counts[i] < bound]
        pool, remaining = sum([weights[i] for i in candidates]), surplus
        for i in candidates:
            extra = min(bound - counts[i], max(1, remaining * weights[i] // pool), surplus)
            counts[i] = counts[i] + extra
            surplus = surplus - extra
    return np.array([bound] + counts)


def uneven(own_key, number_of, total, limit, lean):
    if number_of == 2:
        one = jax.random.randint(own_key, (), max(1, total - limit), min(limit, total - 1) + 1)
        return jnp.stack([one, total - one])
    lengths = jnp.asarray(split_up(number_of, total, limit, lean), jnp.int32)
    couples = (number_of - 1) // 2
    donor, taker = lengths[1:1 + 2 * couples:2], lengths[2:2 + 2 * couples:2]
    room = jnp.minimum(donor - 1, limit - taker)
    passed = jax.random.randint(jax.random.fold_in(own_key, 1), (couples,), 0, 1 << 20) % (room + 1)
    lengths = lengths.at[1:1 + 2 * couples:2].set(donor - passed).at[2:2 + 2 * couples:2].set(taker + passed)
    return lengths[jax.random.permutation(jax.random.fold_in(own_key, 2), number_of)]


def normal_values(stream_key, dims, spread, reach, shards=(), kind=jnp.bfloat16):
    drawn = spread * jax.random.normal(stream_key, dims, jnp.float32)
    if shards:
        drawn = drawn * block_scale(stream_key, dims, shards, -0.22, 0.18)
    return jnp.clip(drawn, -reach, reach).astype(kind)


def setup_inputs(seed: int = 0) -> dict:
    seeds = jax.random.split(jax.random.key(seed), 7)
    return {
        "hidden_states": draw_hidden_states(jax.random.fold_in(seeds[6], 71), 0),
        "queries": draw_queries(jax.random.fold_in(seeds[6], 71), 0),
        "keys": normal_values(seeds[2], (PACKED_TOKENS, KEY_VALUE_HEADS * HEAD_SIZE), 1.0, 6.0, ((0, 64), (1, 8))),
        "values": normal_values(seeds[3], (PACKED_TOKENS, KEY_VALUE_HEADS * HEAD_SIZE), 1.0, 6.0, ((0, 64), (1, 8))),
        "output_gradient": draw_output_gradient(jax.random.fold_in(seeds[6], 71), 0),
        "doc_blocks": uneven(seeds[5], DOCS, PACKED_TOKENS // BLOCK_TOKENS, REACH * TOK_DEV // BLOCK_TOKENS, 2).astype(jnp.int32),
    }


def doc_ids(positions, doc_blocks):
    ends = jnp.cumsum(doc_blocks.astype(jnp.int32)) * BLOCK_TOKENS
    found = lax.optimization_barrier(jnp.sum((positions[:, None] >= ends[None, :]).astype(jnp.int32), axis=1))
    return jnp.where(positions >= 0, found, -1).astype(jnp.int32)

def undo_rotary(grads, positions):
    half = HEAD_SIZE // 2
    freqs = 500000.0 ** (-(jnp.arange(half, dtype=jnp.float32) * 2.0) / HEAD_SIZE)
    angles = positions.astype(jnp.float32)[:, None] * freqs[None, :]
    cosine = jnp.concatenate([jnp.cos(angles), jnp.cos(angles)], axis=-1)[:, None, :]
    sine = jnp.concatenate([jnp.sin(angles), jnp.sin(angles)], axis=-1)[:, None, :]
    shaped = grads.reshape(grads.shape[0], -1, HEAD_SIZE)
    rotated = jnp.concatenate([-shaped[..., half:], shaped[..., :half]], axis=-1)
    return (shaped * cosine - rotated * sine).reshape(grads.shape)

def reference(hidden_states, queries, keys, values, output_gradient, doc_blocks):
    query_group = QUERY_HEADS // KEY_VALUE_HEADS
    window_extent = REACH * TOK_DEV
    window_width = window_extent + BLOCK_TOKENS
    scale = HEAD_SIZE ** (-0.5)
    leading_edge = jnp.zeros((window_extent, KEY_VALUE_HEADS * HEAD_SIZE), jnp.bfloat16)
    keys_padded = jnp.concatenate([leading_edge, keys], axis=0)
    values_padded = jnp.concatenate([leading_edge, values], axis=0)

    def step(carry, index):
        key_running, value_running = carry
        begin_offset = (index * BLOCK_TOKENS).astype(jnp.int32)
        query_block = lax.dynamic_slice_in_dim(queries, begin_offset, BLOCK_TOKENS, 0).reshape(BLOCK_TOKENS, KEY_VALUE_HEADS, query_group, HEAD_SIZE).astype(jnp.float32)
        gradient_block = lax.dynamic_slice_in_dim(output_gradient, begin_offset, BLOCK_TOKENS, 0).reshape(BLOCK_TOKENS, KEY_VALUE_HEADS, query_group, HEAD_SIZE).astype(jnp.float32)
        key_window = lax.dynamic_slice_in_dim(keys_padded, begin_offset, window_width, 0).reshape(window_width, KEY_VALUE_HEADS, HEAD_SIZE).astype(jnp.float32)
        value_window = lax.dynamic_slice_in_dim(values_padded, begin_offset, window_width, 0).reshape(window_width, KEY_VALUE_HEADS, HEAD_SIZE).astype(jnp.float32)
        q_pos = begin_offset + jnp.arange(BLOCK_TOKENS, dtype=jnp.int32)
        k_pos = begin_offset - window_extent + jnp.arange(window_width, dtype=jnp.int32)
        mask = (doc_ids(q_pos, doc_blocks)[:, None] == doc_ids(k_pos, doc_blocks)[None, :]) & (k_pos[None, :] <= q_pos[:, None]) & (k_pos[None, :] >= 0)
        score = jnp.einsum('bkgd,wkd->kgbw', query_block, key_window) * scale
        top = lax.optimization_barrier(jnp.max(jnp.where(mask, score, -1e+30), axis=-1, keepdims=True))
        total = lax.optimization_barrier(jnp.sum(jnp.where(mask, jnp.exp(score - top), 0.0), axis=-1, keepdims=True))
        lse = top + jnp.log(total)
        prob = jnp.where(mask, jnp.exp(score - lse), 0.0)
        prob16 = prob.astype(jnp.bfloat16)
        attn_out = jnp.einsum('kgbw,wkd->bkgd', prob16.astype(jnp.float32), value_window).astype(jnp.bfloat16)
        delta = lax.optimization_barrier(jnp.sum(gradient_block * attn_out.astype(jnp.float32), axis=-1))
        delta = jnp.transpose(delta, (1, 2, 0))[..., None]
        dprob = jnp.einsum('bkgd,wkd->kgbw', gradient_block, value_window)
        dscore = (prob * (dprob - delta)).astype(jnp.bfloat16)
        key_portion = jnp.einsum('kgbw,bkgd->wkd', dscore.astype(jnp.float32), query_block) * scale
        value_portion = jnp.einsum('kgbw,bkgd->wkd', prob16.astype(jnp.float32), gradient_block)
        key_previous = lax.dynamic_slice_in_dim(key_running, begin_offset, window_width, 0)
        value_previous = lax.dynamic_slice_in_dim(value_running, begin_offset, window_width, 0)
        key_running = lax.dynamic_update_slice_in_dim(key_running, key_previous + key_portion.reshape(window_width, KEY_VALUE_HEADS * HEAD_SIZE), begin_offset, 0)
        value_running = lax.dynamic_update_slice_in_dim(value_running, value_previous + value_portion.reshape(window_width, KEY_VALUE_HEADS * HEAD_SIZE), begin_offset, 0)
        return ((key_running, value_running), None)
    zero_filled = jnp.zeros((window_extent + PACKED_TOKENS, KEY_VALUE_HEADS * HEAD_SIZE), jnp.float32)
    (key_running, value_running), _ = lax.scan(step, (zero_filled, zero_filled), jnp.arange(PACKED_TOKENS // BLOCK_TOKENS, dtype=jnp.int32))
    positions = jnp.arange(PACKED_TOKENS, dtype=jnp.int32)
    pre_key = undo_rotary(key_running[window_extent:], positions).astype(jnp.bfloat16)
    pre_value = value_running[window_extent:].astype(jnp.bfloat16)
    key_gradient = jnp.dot(hidden_states.T, pre_key, preferred_element_type=jnp.float32)
    value_gradient = jnp.dot(hidden_states.T, pre_value, preferred_element_type=jnp.float32)
    squared_mean = (jnp.sum(key_gradient * key_gradient) + jnp.sum(value_gradient * value_gradient)) / (2.0 * MODEL_WIDTH * KEY_VALUE_HEADS * HEAD_SIZE)
    factor = 1.0 / jnp.sqrt(squared_mean + 1e-06)
    return (key_gradient * factor, value_gradient * factor)
```

```python
import functools

import jax
import jax.numpy as jnp
from jax import lax
from jax.experimental import pallas as pl
from jax.experimental.pallas import tpu as pltpu
from jax.sharding import Mesh, PartitionSpec as P

MODEL_WIDTH = 8192
QUERY_HEADS = 64
KEY_VALUE_HEADS = 8
HEAD_SIZE = 128
BLOCK_TOKENS = 128
GROUP = QUERY_HEADS // KEY_VALUE_HEADS
ROWS = GROUP * BLOCK_TOKENS
PLANES = 7
SIDE = 4
NEGATIVE = -1e30
SCALE = HEAD_SIZE ** (-0.5)
LOG2E = 1.4426950408889634
EXP_SCALE = SCALE * LOG2E
Z = ("z_hi", "z_lo")
CTX = ("z_hi", "z_lo", "y")

NT = (((1,), (1,)), ((), ()))
NN = (((1,), (0,)), ((), ()))
TN = (((0,), (0,)), ((), ()))


def axis_total(axis):
    names = axis if isinstance(axis, tuple) else (axis,)
    total = 1
    for name in names:
        total *= lax.axis_size(name)
    return total


def rotate(value, axis, steps):
    count = axis_total(axis)
    return lax.ppermute(value, axis, [(at, (at + steps) % count) for at in range(count)])


def stack_heads(src_ref, dst_ref):
    for head in range(GROUP):
        dst_ref[head * BLOCK_TOKENS:(head + 1) * BLOCK_TOKENS, :] = src_ref[
            :, head * HEAD_SIZE:(head + 1) * HEAD_SIZE
        ]


def causal_mask():
    token = lax.broadcasted_iota(jnp.int32, (BLOCK_TOKENS, ROWS), 0)
    query = lax.broadcasted_iota(jnp.int32, (BLOCK_TOKENS, ROWS), 1)
    return token <= (query & (BLOCK_TOKENS - 1))


def block_valid(info_ref, plane, turn):
    row = info_ref[2]
    other = (row + turn) & (SIDE - 1)
    offset = SIDE * plane + row - other
    return (offset >= 0) & (info_ref[0] - offset >= info_ref[1])


def stats_kernel(turn, info_ref, q_ref, g_ref, kv_ref, *rest):
    if turn == 0:
        out_ref, qs_ref, gs_ref = rest
        out_ref[0:1, :] = jnp.full((1, ROWS), NEGATIVE, jnp.float32)
        out_ref[1:, :] = jnp.zeros((7, ROWS), jnp.float32)
    else:
        in_ref, out_ref, qs_ref, gs_ref = rest
        out_ref[...] = in_ref[...]
    stack_heads(q_ref, qs_ref)
    stack_heads(g_ref, gs_ref)
    for plane in range(PLANES):

        @pl.when(block_valid(info_ref, plane, turn))
        def _():
            score = lax.dot_general(
                kv_ref[plane, :, :HEAD_SIZE], qs_ref[...], NT, preferred_element_type=jnp.float32
            )
            if turn == 0 and plane == 0:
                score = jnp.where(causal_mask(), score, NEGATIVE)
            dprob = lax.dot_general(
                kv_ref[plane, :, HEAD_SIZE:], gs_ref[...], NT, preferred_element_type=jnp.float32
            )
            old = out_ref[0:1, :]
            top = jnp.maximum(old, jnp.max(score, axis=0, keepdims=True))
            weight = jnp.exp2((score - top) * EXP_SCALE)
            keep = jnp.exp2((old - top) * EXP_SCALE)
            out_ref[0:1, :] = top
            out_ref[1:2, :] = out_ref[1:2, :] * keep + jnp.sum(weight, axis=0, keepdims=True)
            out_ref[2:3, :] = out_ref[2:3, :] * keep + jnp.sum(
                weight * dprob, axis=0, keepdims=True
            )


def grads_kernel(turn, info_ref, q_ref, g_ref, kv_ref, stats_ref, out_ref, qs_ref, gs_ref):
    stack_heads(q_ref, qs_ref)
    stack_heads(g_ref, gs_ref)
    total = stats_ref[1:2, :]
    lse = stats_ref[0:1, :] * EXP_SCALE + jnp.log2(total)
    delta = stats_ref[2:3, :] / total
    for plane in range(PLANES):
        valid = block_valid(info_ref, plane, turn)

        @pl.when(valid)
        def _():
            score = lax.dot_general(
                kv_ref[plane, :, :HEAD_SIZE], qs_ref[...], NT, preferred_element_type=jnp.float32
            )
            dprob = lax.dot_general(
                kv_ref[plane, :, HEAD_SIZE:], gs_ref[...], NT, preferred_element_type=jnp.float32
            )
            prob = jnp.exp2(score * EXP_SCALE - lse)
            if turn == 0 and plane == 0:
                prob = jnp.where(causal_mask(), prob, 0.0)
            dscore = (prob * (dprob - delta)).astype(jnp.bfloat16)
            key_part = lax.dot_general(
                dscore, qs_ref[...], NN, preferred_element_type=jnp.float32
            )
            value_part = lax.dot_general(
                prob.astype(jnp.bfloat16), gs_ref[...], NN, preferred_element_type=jnp.float32
            )
            out_ref[plane, :, :HEAD_SIZE] = (key_part * SCALE).astype(out_ref.dtype)
            out_ref[plane, :, HEAD_SIZE:] = value_part.astype(out_ref.dtype)

        @pl.when(jnp.logical_not(valid))
        def _():
            out_ref[plane] = jnp.zeros(out_ref.shape[1:], out_ref.dtype)


SMEM_SPEC = pl.BlockSpec(memory_space=pltpu.SMEM)
VMEM_SPEC = pl.BlockSpec(memory_space=pltpu.VMEM)
STACKS = [
    pltpu.VMEM((ROWS, HEAD_SIZE), jnp.bfloat16),
    pltpu.VMEM((ROWS, HEAD_SIZE), jnp.bfloat16),
]
PARAMS = pltpu.CompilerParams(vmem_limit_bytes=48 * 1024 * 1024)


def stats_pass(turn, info, q, g, kv, stats):
    extra = [] if turn == 0 else [stats]
    return pl.pallas_call(
        functools.partial(stats_kernel, turn),
        out_shape=jax.ShapeDtypeStruct((8, ROWS), jnp.float32),
        in_specs=[SMEM_SPEC] + [VMEM_SPEC] * (3 + len(extra)),
        out_specs=VMEM_SPEC,
        scratch_shapes=STACKS,
        compiler_params=PARAMS,
        name=f"stats{turn}",
    )(info, q, g, kv, *extra)


def grads_pass(turn, info, q, g, kv, stats):
    return pl.pallas_call(
        functools.partial(grads_kernel, turn),
        out_shape=jax.ShapeDtypeStruct((PLANES, BLOCK_TOKENS, 2 * HEAD_SIZE), jnp.bfloat16),
        in_specs=[SMEM_SPEC] + [VMEM_SPEC] * 4,
        out_specs=VMEM_SPEC,
        scratch_shapes=STACKS,
        compiler_params=PARAMS,
        name=f"grads{turn}",
    )(info, q, g, kv, stats)


def pick_kernel(pick_ref, src_ref, out_ref):
    out_ref[0] = src_ref[...]


def pick_features(hidden, head):
    pick = jnp.stack([2 * (head % 2), head // 2]).astype(jnp.int32)
    spec = pltpu.PrefetchScalarGridSpec(
        num_scalar_prefetch=1,
        grid=(SIDE, 2),
        in_specs=[
            pl.BlockSpec(
                (BLOCK_TOKENS, 128),
                lambda lo, half, pick: (0, (pick[0] + half) * 16 + lo * 4 + pick[1]),
            )
        ],
        out_specs=pl.BlockSpec((1, BLOCK_TOKENS, 128), lambda lo, half, pick: (lo, 0, half)),
    )
    return pl.pallas_call(
        pick_kernel,
        out_shape=jax.ShapeDtypeStruct((SIDE, BLOCK_TOKENS, 256), hidden.dtype),
        grid_spec=spec,
        name="pick",
    )(pick, hidden)


def rotary_tables(positions):
    half = HEAD_SIZE // 2
    freqs = 500000.0 ** (-(jnp.arange(half, dtype=jnp.float32) * 2.0) / HEAD_SIZE)
    angles = positions.astype(jnp.float32)[:, None] * freqs[None, :]
    cosine, sine = jnp.cos(angles), jnp.sin(angles)
    return jnp.concatenate([cosine, cosine], -1), jnp.concatenate([sine, sine], -1)


def exchange(value, axis):
    return lax.all_to_all(value, axis, split_axis=0, concat_axis=0, tiled=True)


def small_sum(value, axis):
    count = axis_total(axis)
    spread = jnp.broadcast_to(value, (count, 8, 128))
    return jnp.sum(exchange(spread, axis), axis=0)[0:1, 0:1]


def per_device(hidden, queries, keys, values, output_gradient, doc_blocks):
    z = lax.axis_index(Z)
    row = lax.axis_index("y")
    head = lax.axis_index("head")
    here = SIDE * z + row
    ends = jnp.cumsum(doc_blocks)
    first = jnp.max(jnp.where(ends <= here, ends, 0))
    info = jnp.stack([here, first, row]).astype(jnp.int32)
    f32 = jnp.float32

    own = jnp.concatenate([keys, values], axis=1)[None]
    four = rotate(own, Z, 4)
    even = jnp.concatenate([own, four])
    two = rotate(even, Z, 2)
    odd = rotate(jnp.concatenate([own, two[0:1], four]), Z, 1)
    column = jnp.concatenate([own, odd[0:1], two[0:1], odd[1:2], four, odd[2:3], two[1:2]])

    columns = [column] + [rotate(column, "y", -turn) for turn in (1, 2, 3)]

    picked = pick_features(hidden, head)
    picked, _ = lax.optimization_barrier((picked, odd))
    tokens = exchange(picked, "z_lo")
    features = lax.all_gather(tokens.reshape(SIDE * BLOCK_TOKENS, 256), "head", axis=0)

    stats = None
    for turn in range(4):
        stats = stats_pass(turn, info, queries, output_gradient, columns[turn], stats)
    summed = None
    parts = {}
    for turn in (1, 2, 3, 0):
        part = grads_pass(turn, info, queries, output_gradient, columns[turn], stats)
        parts[turn] = rotate(part, "y", turn) if turn else part
    summed = sum(parts[turn].astype(f32) for turn in (0, 1, 2, 3))

    odd_back = rotate(
        jnp.concatenate([summed[1:2], summed[3:4], summed[5:6]]).astype(jnp.bfloat16), Z, -1
    ).astype(f32)
    s0 = summed[0] + odd_back[0]
    s2 = summed[2] + odd_back[1]
    s4 = summed[4] + odd_back[2]
    two_back = rotate(jnp.stack([s2, summed[6]]).astype(jnp.bfloat16), Z, -2).astype(f32)
    s0 = s0 + two_back[0]
    s4 = s4 + two_back[1]
    four_back = rotate(s4.astype(jnp.bfloat16), Z, -4).astype(f32)
    s0 = s0 + four_back

    cosine, sine = rotary_tables(here * BLOCK_TOKENS + jnp.arange(BLOCK_TOKENS))
    key_grad = s0[:, :HEAD_SIZE]
    half = HEAD_SIZE // 2
    turned = jnp.concatenate([-key_grad[:, half:], key_grad[:, :half]], axis=-1)
    pre = jnp.concatenate([key_grad * cosine - turned * sine, s0[:, HEAD_SIZE:]], axis=1)
    pre = pre.astype(jnp.bfloat16)
    gathered = exchange(jnp.broadcast_to(pre, (SIDE,) + pre.shape), "z_lo")
    gathered = gathered.reshape(SIDE * BLOCK_TOKENS, 2 * HEAD_SIZE)

    weight = lax.dot_general(
        features, gathered, (((1,), (0,)), ((), ())), preferred_element_type=f32
    ).astype(jnp.bfloat16)
    weight = exchange(weight.reshape(SIDE, SIDE * BLOCK_TOKENS, 256), "y")
    weight = jnp.sum(weight.astype(f32), axis=0).astype(jnp.bfloat16)
    weight = exchange(weight.reshape(SIDE, BLOCK_TOKENS, 256), "z_hi")
    weight = jnp.sum(weight.astype(f32), axis=0)

    squares = jnp.sum(weight * weight).reshape(1, 1)
    squares = lax.psum(squares, "z_lo")
    squares = lax.psum(squares, "z_hi")
    squares = small_sum(squares, "y")
    squares = small_sum(squares, "head")
    mean_square = squares / (2.0 * MODEL_WIDTH * KEY_VALUE_HEADS * HEAD_SIZE)
    factor = 1.0 / jnp.sqrt(mean_square + 1e-06)
    scaled = weight * factor
    return (scaled[:, :HEAD_SIZE], scaled[:, HEAD_SIZE:])


def solution(mesh):
    devices = mesh.devices.reshape(4, 4, 4, 8)
    split = Mesh(devices, ("z_hi", "z_lo", "y", "head"))
    placed = (P(CTX, None),) + (P(CTX, "head"),) * 4 + (P(),)
    return jax.shard_map(
        per_device,
        mesh=split,
        in_specs=placed,
        out_specs=(P(CTX, "head"), P(CTX, "head")),
        check_vma=False,
    )
```

```python
import functools

import jax
import jax.numpy as jnp
from jax import lax
from jax.experimental import pallas as pl
from jax.experimental.pallas import tpu as pltpu
from jax.sharding import Mesh, PartitionSpec as P

MODEL_WIDTH = 8192
QUERY_HEADS = 64
KEY_VALUE_HEADS = 8
HEAD_SIZE = 128
BLOCK_TOKENS = 128
GROUP = QUERY_HEADS // KEY_VALUE_HEADS
ROWS = GROUP * BLOCK_TOKENS
PLANES = 7
SIDE = 4
STATS = 2
ODD = (1, 3, 5)
EVEN = (0, 2, 4, 6)
NEGATIVE = -1e30
SCALE = HEAD_SIZE ** (-0.5)
LOG2E = 1.4426950408889634
EXP_SCALE = SCALE * LOG2E
Z = ("z_hi", "z_lo")
CTX = ("z_hi", "z_lo", "y")

NT = (((1,), (1,)), ((), ()))
NN = (((1,), (0,)), ((), ()))
TN = (((0,), (0,)), ((), ()))


def axis_total(axis):
    names = axis if isinstance(axis, tuple) else (axis,)
    total = 1
    for name in names:
        total *= lax.axis_size(name)
    return total


def rotate(value, axis, steps):
    count = axis_total(axis)
    return lax.ppermute(value, axis, [(at, (at + steps) % count) for at in range(count)])


def stack_heads(src_ref, which, dst_ref):
    for head in range(GROUP):
        dst_ref[head * BLOCK_TOKENS:(head + 1) * BLOCK_TOKENS, :] = src_ref[
            0, which, :, head * HEAD_SIZE:(head + 1) * HEAD_SIZE
        ]


def causal_mask(offset):
    token = lax.broadcasted_iota(jnp.int32, (BLOCK_TOKENS, ROWS), 0)
    query = lax.broadcasted_iota(jnp.int32, (BLOCK_TOKENS, ROWS), 1)
    return token <= (query & (BLOCK_TOKENS - 1)) + BLOCK_TOKENS * offset


def block_offset(info_ref, plane, query_row):
    offset = SIDE * plane + query_row - info_ref[1]
    position = SIDE * info_ref[0] + query_row
    return offset, (offset >= 0) & (position - offset >= info_ref[2 + query_row])


def stats_kernel(info_ref, qg_ref, kv_ref, out_ref, qs_ref, gs_ref, run_ref):
    query_row = pl.program_id(0)
    run_ref[0:1, :] = jnp.full((1, ROWS), NEGATIVE, jnp.float32)
    run_ref[1:, :] = jnp.zeros((7, ROWS), jnp.float32)
    stack_heads(qg_ref, 0, qs_ref)
    stack_heads(qg_ref, 1, gs_ref)
    for plane in range(PLANES):
        offset, valid = block_offset(info_ref, plane, query_row)

        @pl.when(valid)
        def _():
            score = lax.dot_general(
                kv_ref[plane, :, :HEAD_SIZE], qs_ref[...], NT, preferred_element_type=jnp.float32
            )
            if plane == 0:
                score = jnp.where(causal_mask(offset), score, NEGATIVE)
            dprob = lax.dot_general(
                kv_ref[plane, :, HEAD_SIZE:], gs_ref[...], NT, preferred_element_type=jnp.float32
            )
            old = run_ref[0:1, :]
            top = jnp.maximum(old, jnp.max(score, axis=0, keepdims=True))
            weight = jnp.exp2((score - top) * EXP_SCALE)
            keep = jnp.exp2((old - top) * EXP_SCALE)
            run_ref[0:1, :] = top
            run_ref[1:2, :] = run_ref[1:2, :] * keep + jnp.sum(weight, axis=0, keepdims=True)
            run_ref[2:3, :] = run_ref[2:3, :] * keep + jnp.sum(
                weight * dprob, axis=0, keepdims=True
            )
    total = run_ref[1:2, :]
    some = total > 0.0
    safe = jnp.where(some, total, 1.0)
    out_ref[0, 0:1, :] = jnp.where(
        some, run_ref[0:1, :] * EXP_SCALE + jnp.log2(safe), NEGATIVE
    )
    out_ref[0, 1:2, :] = run_ref[2:3, :] / safe


def grads_kernel(
    planes, info_ref, qg_ref, kv_ref, stats_ref, out_ref, qs_ref, gs_ref, acc_ref
):
    query_row = pl.program_id(0)

    @pl.when(query_row == 0)
    def _():
        acc_ref[...] = jnp.zeros(acc_ref.shape, jnp.float32)

    stack_heads(qg_ref, 0, qs_ref)
    stack_heads(qg_ref, 1, gs_ref)
    parts = [stats_ref[source, 0, 0:1, :] for source in range(SIDE)]
    top = functools.reduce(jnp.maximum, parts)
    shares = [jnp.exp2(part - top) for part in parts]
    total = sum(shares)
    lse = top + jnp.log2(total)
    inner = sum(stats_ref[source, 0, 1:2, :] * shares[source] for source in range(SIDE))
    delta = inner / total
    for slot, plane in enumerate(planes):
        offset, valid = block_offset(info_ref, plane, query_row)

        @pl.when(valid)
        def _():
            score = lax.dot_general(
                kv_ref[plane, :, :HEAD_SIZE], qs_ref[...], NT, preferred_element_type=jnp.float32
            )
            dprob = lax.dot_general(
                kv_ref[plane, :, HEAD_SIZE:], gs_ref[...], NT, preferred_element_type=jnp.float32
            )
            prob = jnp.exp2(score * EXP_SCALE - lse)
            if plane == 0:
                prob = jnp.where(causal_mask(offset), prob, 0.0)
            dscore = (prob * (dprob - delta)).astype(jnp.bfloat16)
            key_part = lax.dot_general(
                dscore, qs_ref[...], NN, preferred_element_type=jnp.float32
            )
            value_part = lax.dot_general(
                prob.astype(jnp.bfloat16), gs_ref[...], NN, preferred_element_type=jnp.float32
            )
            acc_ref[slot, :, :HEAD_SIZE] += key_part * SCALE
            acc_ref[slot, :, HEAD_SIZE:] += value_part

    @pl.when(query_row == SIDE - 1)
    def _():
        out_ref[...] = acc_ref[...].astype(out_ref.dtype)


SMEM_SPEC = pl.BlockSpec(memory_space=pltpu.SMEM)
ROW_SPEC = pl.BlockSpec((1, 2, BLOCK_TOKENS, GROUP * HEAD_SIZE), lambda row: (row, 0, 0, 0))
KV_SHAPE = (PLANES, BLOCK_TOKENS, 2 * HEAD_SIZE)
KV_SPEC = pl.BlockSpec(KV_SHAPE, lambda row: (0, 0, 0))
STACKS = [
    pltpu.VMEM((ROWS, HEAD_SIZE), jnp.bfloat16),
    pltpu.VMEM((ROWS, HEAD_SIZE), jnp.bfloat16),
]
PARAMS = pltpu.CompilerParams(vmem_limit_bytes=40 * 1024 * 1024)


def stats_pass(info, qg, kv):
    return pl.pallas_call(
        stats_kernel,
        grid=(SIDE,),
        out_shape=jax.ShapeDtypeStruct((SIDE, STATS, ROWS), jnp.float32),
        in_specs=[SMEM_SPEC, ROW_SPEC, KV_SPEC],
        out_specs=pl.BlockSpec((1, STATS, ROWS), lambda row: (row, 0, 0)),
        scratch_shapes=STACKS + [pltpu.VMEM((8, ROWS), jnp.float32)],
        compiler_params=PARAMS,
        name="stats",
    )(info, qg, kv)


def grads_pass(planes, dtype, info, qg, kv, stats):
    shape = (len(planes), BLOCK_TOKENS, 2 * HEAD_SIZE)
    return pl.pallas_call(
        functools.partial(grads_kernel, planes),
        grid=(SIDE,),
        out_shape=jax.ShapeDtypeStruct(shape, dtype),
        in_specs=[
            SMEM_SPEC,
            ROW_SPEC,
            KV_SPEC,
            pl.BlockSpec((SIDE, 1, STATS, ROWS), lambda row: (0, row, 0, 0)),
        ],
        out_specs=pl.BlockSpec(shape, lambda row: (0, 0, 0)),
        scratch_shapes=STACKS + [pltpu.VMEM(shape, jnp.float32)],
        compiler_params=PARAMS,
        name="grads" + str(planes[0]),
    )(info, qg, kv, stats)


def pick_kernel(pick_ref, src_ref, out_ref):
    out_ref[0] = src_ref[...]


def pick_features(hidden, head):
    pick = jnp.stack([2 * (head % 2), head // 2]).astype(jnp.int32)
    spec = pltpu.PrefetchScalarGridSpec(
        num_scalar_prefetch=1,
        grid=(SIDE, 2),
        in_specs=[
            pl.BlockSpec(
                (BLOCK_TOKENS, 128),
                lambda lo, half, pick: (0, (pick[0] + half) * 16 + lo * 4 + pick[1]),
            )
        ],
        out_specs=pl.BlockSpec((1, BLOCK_TOKENS, 128), lambda lo, half, pick: (lo, 0, half)),
    )
    return pl.pallas_call(
        pick_kernel,
        out_shape=jax.ShapeDtypeStruct((SIDE, BLOCK_TOKENS, 256), hidden.dtype),
        grid_spec=spec,
        name="pick",
    )(pick, hidden)


def rotary_tables(positions):
    half = HEAD_SIZE // 2
    freqs = 500000.0 ** (-(jnp.arange(half, dtype=jnp.float32) * 2.0) / HEAD_SIZE)
    angles = positions.astype(jnp.float32)[:, None] * freqs[None, :]
    cosine, sine = jnp.cos(angles), jnp.sin(angles)
    return jnp.concatenate([cosine, cosine], -1), jnp.concatenate([sine, sine], -1)


def exchange(value, axis):
    return lax.all_to_all(value, axis, split_axis=0, concat_axis=0, tiled=True)


def small_sum(value, axis):
    count = axis_total(axis)
    spread = jnp.broadcast_to(value, (count, 8, 128))
    return jnp.sum(exchange(spread, axis), axis=0)[0:1, 0:1]


def per_device(hidden, queries, keys, values, output_gradient, doc_blocks):
    z = lax.axis_index(Z)
    row = lax.axis_index("y")
    head = lax.axis_index("head")
    ends = jnp.cumsum(doc_blocks)
    rows = SIDE * z + jnp.arange(SIDE)
    firsts = jnp.max(jnp.where(ends[None, :] <= rows[:, None], ends[None, :], 0), axis=1)
    info = jnp.concatenate([jnp.stack([z, row]), firsts]).astype(jnp.int32)
    here = SIDE * z + row
    f32 = jnp.float32

    paired = lax.all_gather(jnp.stack([queries, output_gradient]), "y")
    paired = pltpu.with_memory_space_constraint(paired, pltpu.HBM)

    own = jnp.concatenate([keys, values], axis=1)[None]
    four = rotate(own, Z, 4)
    even = jnp.concatenate([own, four])
    two = rotate(even, Z, 2)
    odd = rotate(jnp.concatenate([own, two[0:1], four]), Z, 1)
    column = jnp.concatenate([own, odd[0:1], two[0:1], odd[1:2], four, odd[2:3], two[1:2]])

    picked = pick_features(hidden, head)
    picked, _ = lax.optimization_barrier((picked, odd))
    tokens = exchange(picked, "z_lo")
    features = lax.all_gather(tokens.reshape(SIDE * BLOCK_TOKENS, 256), "head", axis=0)

    stats = stats_pass(info, paired, column)
    stats = exchange(jnp.broadcast_to(stats, (SIDE,) + stats.shape), "y")
    odd_grads = grads_pass(ODD, jnp.bfloat16, info, paired, column, stats)
    odd_back = rotate(odd_grads, Z, -1)
    even_grads = grads_pass(EVEN, f32, info, paired, column, stats)
    odd_back = odd_back.astype(f32)
    s0 = even_grads[0] + odd_back[0]
    s2 = even_grads[1] + odd_back[1]
    s4 = even_grads[2] + odd_back[2]
    two_back = rotate(jnp.stack([s2, even_grads[3]]).astype(jnp.bfloat16), Z, -2).astype(f32)
    s0 = s0 + two_back[0]
    s4 = s4 + two_back[1]
    four_back = rotate(s4.astype(jnp.bfloat16), Z, -4).astype(f32)
    s0 = s0 + four_back

    cosine, sine = rotary_tables(here * BLOCK_TOKENS + jnp.arange(BLOCK_TOKENS))
    key_grad = s0[:, :HEAD_SIZE]
    half = HEAD_SIZE // 2
    turned = jnp.concatenate([-key_grad[:, half:], key_grad[:, :half]], axis=-1)
    pre = jnp.concatenate([key_grad * cosine - turned * sine, s0[:, HEAD_SIZE:]], axis=1)
    pre = pre.astype(jnp.bfloat16)
    gathered = exchange(jnp.broadcast_to(pre, (SIDE,) + pre.shape), "z_lo")
    gathered = gathered.reshape(SIDE * BLOCK_TOKENS, 2 * HEAD_SIZE)

    weight = lax.dot_general(
        features, gathered, (((1,), (0,)), ((), ())), preferred_element_type=f32
    ).astype(jnp.bfloat16)
    weight = exchange(weight.reshape(SIDE, SIDE * BLOCK_TOKENS, 256), "y")
    weight = jnp.sum(weight.astype(f32), axis=0).astype(jnp.bfloat16)
    weight = exchange(weight.reshape(SIDE, BLOCK_TOKENS, 256), "z_hi")
    weight = jnp.sum(weight.astype(f32), axis=0)

    squares = jnp.sum(weight * weight).reshape(1, 1)
    squares = small_sum(squares, ("y", "head"))
    squares = small_sum(squares, Z)
    mean_square = squares / (2.0 * MODEL_WIDTH * KEY_VALUE_HEADS * HEAD_SIZE)
    factor = 1.0 / jnp.sqrt(mean_square + 1e-06)
    scaled = weight * factor
    return (scaled[:, :HEAD_SIZE], scaled[:, HEAD_SIZE:])


def solution(mesh):
    devices = mesh.devices.reshape(4, 4, 4, 8)
    split = Mesh(devices, ("z_hi", "z_lo", "y", "head"))
    placed = (P(CTX, None),) + (P(CTX, "head"),) * 4 + (P(),)
    return jax.shard_map(
        per_device,
        mesh=split,
        in_specs=placed,
        out_specs=(P(CTX, "head"), P(CTX, "head")),
        check_vma=False,
    )
```

```python
import functools

import jax
import jax.numpy as jnp
from jax import lax
from jax.experimental import pallas as pl
from jax.experimental.pallas import tpu as pltpu
from jax.sharding import Mesh, PartitionSpec as P

MODEL_WIDTH = 8192
QUERY_HEADS = 64
KEY_VALUE_HEADS = 8
HEAD_SIZE = 128
BLOCK_TOKENS = 128
GROUP = QUERY_HEADS // KEY_VALUE_HEADS
ROWS = GROUP * BLOCK_TOKENS
PLANES = 7
SIDE = 4
STATS = 2
ORDER = (0, 2, 4, 6, 1, 3, 5)
EVEN_GROUPS = ((0, 2), (2, 4))
ODD_GROUPS = ((4, 6), (6, 7))
NEGATIVE = -1e30
SCALE = HEAD_SIZE ** (-0.5)
LOG2E = 1.4426950408889634
EXP_SCALE = SCALE * LOG2E
Z = ("z_hi", "z_lo")
CTX = ("z_hi", "z_lo", "y")

NT = (((1,), (1,)), ((), ()))
NN = (((1,), (0,)), ((), ()))
TN = (((0,), (0,)), ((), ()))


def axis_total(axis):
    names = axis if isinstance(axis, tuple) else (axis,)
    total = 1
    for name in names:
        total *= lax.axis_size(name)
    return total


def rotate(value, axis, steps):
    count = axis_total(axis)
    return lax.ppermute(value, axis, [(at, (at + steps) % count) for at in range(count)])


def stack_heads(row_ref, which, dst_ref):
    for head in range(GROUP):
        dst_ref[head * BLOCK_TOKENS:(head + 1) * BLOCK_TOKENS, :] = row_ref[
            0, which, :, head * HEAD_SIZE:(head + 1) * HEAD_SIZE
        ]


def causal_mask(offset):
    token = lax.broadcasted_iota(jnp.int32, (BLOCK_TOKENS, ROWS), 0)
    query = lax.broadcasted_iota(jnp.int32, (BLOCK_TOKENS, ROWS), 1)
    return token <= (query & (BLOCK_TOKENS - 1)) + BLOCK_TOKENS * offset


def block_offset(info_ref, plane, query_row):
    offset = SIDE * plane + query_row - info_ref[1]
    position = SIDE * info_ref[0] + query_row
    return offset, (offset >= 0) & (position - offset >= info_ref[2 + query_row])


def group_valid(info_ref, first, last, query_row):
    return [block_offset(info_ref, ORDER[slot], query_row) for slot in range(first, last)]


def masked(value, checks, first, fill):
    parts = []
    for index, (offset, valid) in enumerate(checks):
        part = value[index * BLOCK_TOKENS:(index + 1) * BLOCK_TOKENS]
        keep = valid if ORDER[first + index] else valid & causal_mask(offset)
        parts.append(jnp.where(keep, part, fill))
    return parts[0] if len(parts) == 1 else jnp.concatenate(parts, axis=0)


def products(kv_ref, first, last, qs, gs):
    rows = (last - first) * BLOCK_TOKENS
    key = kv_ref[first:last, :, :HEAD_SIZE].reshape(rows, HEAD_SIZE)
    value = kv_ref[first:last, :, HEAD_SIZE:].reshape(rows, HEAD_SIZE)
    score = lax.dot_general(key, qs, NT, preferred_element_type=jnp.float32)
    dprob = lax.dot_general(value, gs, NT, preferred_element_type=jnp.float32)
    return score, dprob


def stats_kernel(info_ref, row_ref, kv_ref, out_ref, qs_ref, gs_ref, run_ref):
    query_row = pl.program_id(0)
    stack_heads(row_ref, 0, qs_ref)
    stack_heads(row_ref, 1, gs_ref)
    run_ref[0:1, :] = jnp.full((1, ROWS), NEGATIVE, jnp.float32)
    run_ref[1:, :] = jnp.zeros((7, ROWS), jnp.float32)
    for first, last in EVEN_GROUPS + ODD_GROUPS:
        checks = group_valid(info_ref, first, last, query_row)

        @pl.when(functools.reduce(jnp.logical_or, [valid for _, valid in checks]))
        def _():
            score, dprob = products(kv_ref, first, last, qs_ref[...], gs_ref[...])
            score = masked(score, checks, first, NEGATIVE)
            old = run_ref[0:1, :]
            top = jnp.maximum(old, jnp.max(score, axis=0, keepdims=True))
            weight = jnp.exp2((score - top) * EXP_SCALE)
            keep = jnp.exp2((old - top) * EXP_SCALE)
            run_ref[0:1, :] = top
            run_ref[1:2, :] = run_ref[1:2, :] * keep + jnp.sum(weight, axis=0, keepdims=True)
            run_ref[2:3, :] = run_ref[2:3, :] * keep + jnp.sum(
                weight * dprob, axis=0, keepdims=True
            )

    total = run_ref[1:2, :]
    some = total > 0.0
    safe = jnp.where(some, total, 1.0)
    lse = jnp.where(some, run_ref[0:1, :] * EXP_SCALE + jnp.log2(safe), NEGATIVE)
    mean = run_ref[2:3, :] / safe
    for target in range(SIDE):
        out_ref[target, 0, 0:1, :] = lse
        out_ref[target, 0, 1:2, :] = mean


def grads_kernel(groups, info_ref, row_ref, kv_ref, stats_ref, out_ref, qs_ref, gs_ref, acc_ref):
    query_row = pl.program_id(0)
    base = groups[0][0]

    @pl.when(query_row == 0)
    def _():
        acc_ref[...] = jnp.zeros(acc_ref.shape, jnp.float32)

    stack_heads(row_ref, 0, qs_ref)
    stack_heads(row_ref, 1, gs_ref)
    parts = [stats_ref[source, 0, 0:1, :] for source in range(SIDE)]
    top = functools.reduce(jnp.maximum, parts)
    shares = [jnp.exp2(part - top) for part in parts]
    total = sum(shares)
    lse = top + jnp.log2(total)
    inner = sum(stats_ref[source, 0, 1:2, :] * shares[source] for source in range(SIDE))
    delta = inner / total
    for first, last in groups:
        checks = group_valid(info_ref, first, last, query_row)

        @pl.when(functools.reduce(jnp.logical_or, [valid for _, valid in checks]))
        def _():
            qs, gs = qs_ref[...], gs_ref[...]
            score, dprob = products(kv_ref, first, last, qs, gs)
            prob = masked(jnp.exp2(score * EXP_SCALE - lse), checks, first, 0.0)
            dscore = (prob * (dprob - delta)).astype(jnp.bfloat16)
            key_part = lax.dot_general(dscore, qs, NN, preferred_element_type=jnp.float32)
            value_part = lax.dot_general(
                prob.astype(jnp.bfloat16), gs, NN, preferred_element_type=jnp.float32
            )
            shape = (last - first, BLOCK_TOKENS, HEAD_SIZE)
            at = slice(first - base, last - base)
            acc_ref[at, :, :HEAD_SIZE] += (key_part * SCALE).reshape(shape)
            acc_ref[at, :, HEAD_SIZE:] += value_part.reshape(shape)

    @pl.when(query_row == SIDE - 1)
    def _():
        out_ref[...] = acc_ref[...].astype(out_ref.dtype)


STACKS = [
    pltpu.VMEM((ROWS, HEAD_SIZE), jnp.bfloat16),
    pltpu.VMEM((ROWS, HEAD_SIZE), jnp.bfloat16),
]
PARAMS = pltpu.CompilerParams(vmem_limit_bytes=40 * 1024 * 1024)
ROW_SHAPE = (1, 2, BLOCK_TOKENS, GROUP * HEAD_SIZE)
ROW_SPEC = pl.BlockSpec(ROW_SHAPE, lambda step, info: (step, 0, 0, 0))
STATS_SPEC = pl.BlockSpec((SIDE, 1, STATS, ROWS), lambda step, info: (0, step, 0, 0))


def whole(shape):
    return pl.BlockSpec(shape, lambda step, info: (0,) * len(shape))


def stats_pass(info, rows, kv):
    spec = pltpu.PrefetchScalarGridSpec(
        num_scalar_prefetch=1,
        grid=(SIDE,),
        in_specs=[ROW_SPEC, whole(kv.shape)],
        out_specs=STATS_SPEC,
        scratch_shapes=STACKS + [pltpu.VMEM((8, ROWS), jnp.float32)],
    )
    return pl.pallas_call(
        stats_kernel,
        out_shape=jax.ShapeDtypeStruct((SIDE, SIDE, STATS, ROWS), jnp.float32),
        grid_spec=spec,
        compiler_params=PARAMS,
        name="stats",
    )(info, rows, kv)


def grads_pass(groups, dtype, info, rows, kv, stats):
    shape = (groups[-1][1] - groups[0][0], BLOCK_TOKENS, 2 * HEAD_SIZE)
    spec = pltpu.PrefetchScalarGridSpec(
        num_scalar_prefetch=1,
        grid=(SIDE,),
        in_specs=[ROW_SPEC, whole(kv.shape), STATS_SPEC],
        out_specs=whole(shape),
        scratch_shapes=STACKS + [pltpu.VMEM(shape, jnp.float32)],
    )
    return pl.pallas_call(
        functools.partial(grads_kernel, groups),
        out_shape=jax.ShapeDtypeStruct(shape, dtype),
        grid_spec=spec,
        compiler_params=PARAMS,
        name="grads" + str(groups[0][0]),
    )(info, rows, kv, stats)


def pick_kernel(pick_ref, left_ref, right_ref, out_ref):
    out_ref[0, :, :128] = left_ref[...]
    out_ref[0, :, 128:] = right_ref[...]


def pick_features(hidden, head):
    pick = jnp.stack([2 * (head % 2), head // 2]).astype(jnp.int32)

    def half_spec(half):
        return pl.BlockSpec(
            (BLOCK_TOKENS, 128), lambda lo, pick: (0, (pick[0] + half) * 16 + lo * 4 + pick[1])
        )

    spec = pltpu.PrefetchScalarGridSpec(
        num_scalar_prefetch=1,
        grid=(SIDE,),
        in_specs=[half_spec(0), half_spec(1)],
        out_specs=pl.BlockSpec((1, BLOCK_TOKENS, 256), lambda lo, pick: (lo, 0, 0)),
    )
    return pl.pallas_call(
        pick_kernel,
        out_shape=jax.ShapeDtypeStruct((SIDE, BLOCK_TOKENS, 256), hidden.dtype),
        grid_spec=spec,
        name="pick",
    )(pick, hidden, hidden)


def square_kernel(parts_ref, weight_ref, spread_ref):
    weight = sum(parts_ref[source].astype(jnp.float32) for source in range(SIDE))
    weight_ref[...] = weight
    squares = jnp.sum((weight * weight).reshape(16, 8, 256), axis=0)
    squares = squares[:, :128] + squares[:, 128:]
    spread_ref[...] = jnp.broadcast_to(squares, spread_ref.shape)


def square_pass(parts):
    return pl.pallas_call(
        square_kernel,
        out_shape=(
            jax.ShapeDtypeStruct((BLOCK_TOKENS, 256), jnp.float32),
            jax.ShapeDtypeStruct((32, 8, 128), jnp.float32),
        ),
        name="square",
    )(parts)


def spread_kernel(parts_ref, out_ref):
    out_ref[...] = jnp.broadcast_to(jnp.sum(parts_ref[...], axis=0), out_ref.shape)


def spread_pass(parts):
    return pl.pallas_call(
        spread_kernel, out_shape=jax.ShapeDtypeStruct((16, 8, 128), jnp.float32), name="spread"
    )(parts)


def finish_kernel(parts_ref, weight_ref, key_ref, value_ref):
    total = jnp.sum(jnp.sum(parts_ref[...], axis=0))
    mean_square = total / (2.0 * MODEL_WIDTH * KEY_VALUE_HEADS * HEAD_SIZE)
    factor = 1.0 / jnp.sqrt(jnp.full((1, HEAD_SIZE), mean_square + 1e-06, jnp.float32))
    key_ref[...] = weight_ref[:, :HEAD_SIZE] * factor
    value_ref[...] = weight_ref[:, HEAD_SIZE:] * factor


def finish_pass(parts, weight):
    shape = jax.ShapeDtypeStruct((BLOCK_TOKENS, HEAD_SIZE), jnp.float32)
    return pl.pallas_call(finish_kernel, out_shape=(shape, shape), name="finish")(parts, weight)


def fan_kernel(src_ref, out_ref):
    out_ref[0] = src_ref[...]


def fan_out(tokens, copies):
    rows, width = tokens.shape
    return pl.pallas_call(
        fan_kernel,
        grid=(copies,),
        out_shape=jax.ShapeDtypeStruct((copies, rows, width), tokens.dtype),
        in_specs=[pl.BlockSpec((rows, width), lambda copy: (0, 0))],
        out_specs=pl.BlockSpec((1, rows, width), lambda copy: (copy, 0, 0)),
        name="fan",
    )(tokens)


def rotary_tables(positions):
    half = HEAD_SIZE // 2
    freqs = 500000.0 ** (-(jnp.arange(half, dtype=jnp.float32) * 2.0) / HEAD_SIZE)
    angles = positions.astype(jnp.float32)[:, None] * freqs[None, :]
    cosine, sine = jnp.cos(angles), jnp.sin(angles)
    return jnp.concatenate([cosine, cosine], -1), jnp.concatenate([sine, sine], -1)


def exchange(value, axis):
    return lax.all_to_all(value, axis, split_axis=0, concat_axis=0, tiled=True)


def per_device(hidden, queries, keys, values, output_gradient, doc_blocks):
    z = lax.axis_index(Z)
    row = lax.axis_index("y")
    head = lax.axis_index("head")
    ends = jnp.cumsum(doc_blocks)
    blocks = SIDE * z + jnp.arange(SIDE)
    firsts = jnp.max(jnp.where(ends[None, :] <= blocks[:, None], ends[None, :], 0), axis=1)
    info = jnp.concatenate([jnp.stack([z, row]), firsts]).astype(jnp.int32)
    here = SIDE * z + row
    f32 = jnp.float32

    own = jnp.concatenate([keys, values], axis=1)[None]
    four = rotate(own, Z, 4)
    rows = jnp.stack([queries, output_gradient])
    query_rows = exchange(jnp.broadcast_to(rows, (SIDE,) + rows.shape), "y")
    even = jnp.concatenate([own, four])
    two = rotate(even, Z, 2)
    odd = rotate(jnp.concatenate([own, two[0:1], four]), Z, 1)
    column = jnp.concatenate([own, two[0:1], four, two[1:2], odd])

    picked, odd = lax.optimization_barrier((pick_features(hidden, head), odd))
    tokens = exchange(picked, "z_lo").reshape(SIDE * BLOCK_TOKENS, 256)
    stats = stats_pass(info, query_rows, column)
    tokens, stats = lax.optimization_barrier((tokens, stats))
    stats = exchange(stats, "y")
    tokens, stats = lax.optimization_barrier((fan_out(tokens, 8), stats))
    features = exchange(tokens, "head")
    odd_grads = grads_pass(ODD_GROUPS, jnp.bfloat16, info, query_rows, column, stats)
    odd_back = rotate(odd_grads, Z, -1)
    even_grads = grads_pass(EVEN_GROUPS, f32, info, query_rows, column, stats)
    odd_back = odd_back.astype(f32)
    s0 = even_grads[0] + odd_back[0]
    s2 = even_grads[1] + odd_back[1]
    s4 = even_grads[2] + odd_back[2]
    two_back = rotate(jnp.stack([s2, even_grads[3]]).astype(jnp.bfloat16), Z, -2).astype(f32)
    s0 = s0 + two_back[0]
    s4 = s4 + two_back[1]
    four_back = rotate(s4.astype(jnp.bfloat16), Z, -4)
    features, four_back = lax.optimization_barrier((features, four_back))
    s0 = s0 + four_back.astype(f32)

    cosine, sine = rotary_tables(here * BLOCK_TOKENS + jnp.arange(BLOCK_TOKENS))
    key_grad = s0[:, :HEAD_SIZE]
    half = HEAD_SIZE // 2
    turned = jnp.concatenate([-key_grad[:, half:], key_grad[:, :half]], axis=-1)
    pre = jnp.concatenate([key_grad * cosine - turned * sine, s0[:, HEAD_SIZE:]], axis=1)
    pre = pre.astype(jnp.bfloat16)
    gathered = exchange(jnp.broadcast_to(pre, (SIDE,) + pre.shape), "z_lo")
    gathered = gathered.reshape(SIDE * BLOCK_TOKENS, 2 * HEAD_SIZE)

    weight = lax.dot_general(
        features, gathered, (((1,), (0,)), ((), ())), preferred_element_type=f32
    ).astype(jnp.bfloat16)
    weight = exchange(weight.reshape(SIDE, SIDE * BLOCK_TOKENS, 256), "y")
    weight = jnp.sum(weight.astype(f32), axis=0).astype(jnp.bfloat16)
    weight = exchange(weight.reshape(SIDE, BLOCK_TOKENS, 256), "z_hi")
    weight, spread = square_pass(weight)
    spread = spread_pass(exchange(spread, ("y", "head")))
    return finish_pass(exchange(spread, Z), weight)


def solution(mesh):
    devices = mesh.devices.reshape(4, 4, 4, 8)
    split = Mesh(devices, ("z_hi", "z_lo", "y", "head"))
    placed = (P(CTX, None),) + (P(CTX, "head"),) * 4 + (P(),)
    return jax.shard_map(
        per_device,
        mesh=split,
        in_specs=placed,
        out_specs=(P(CTX, "head"), P(CTX, "head")),
        check_vma=False,
    )
```

```python
import functools

import jax
import jax.numpy as jnp
from jax import lax
from jax.experimental import pallas as pl
from jax.experimental.pallas import tpu as pltpu
from jax.sharding import Mesh, PartitionSpec as P

MODEL_WIDTH = 8192
QUERY_HEADS = 64
KEY_VALUE_HEADS = 8
HEAD_SIZE = 128
BLOCK_TOKENS = 128
GROUP = QUERY_HEADS // KEY_VALUE_HEADS
ROWS = GROUP * BLOCK_TOKENS
PLANES = 7
SIDE = 4
STATS = 2
ORDER = (0, 2, 4, 6, 1, 3, 5)
EVEN_GROUPS = ((0, 4),)
ODD_GROUPS = ((4, 7),)
NEGATIVE = -1e30
SCALE = HEAD_SIZE ** (-0.5)
LOG2E = 1.4426950408889634
EXP_SCALE = SCALE * LOG2E
Z = ("z_hi", "z_lo")
CTX = ("z_hi", "z_lo", "y")

NT = (((1,), (1,)), ((), ()))
NN = (((1,), (0,)), ((), ()))
TN = (((0,), (0,)), ((), ()))


def axis_total(axis):
    names = axis if isinstance(axis, tuple) else (axis,)
    total = 1
    for name in names:
        total *= lax.axis_size(name)
    return total


def rotate(value, axis, steps):
    count = axis_total(axis)
    return lax.ppermute(value, axis, [(at, (at + steps) % count) for at in range(count)])


def stack_heads(row_ref, which, dst_ref):
    for head in range(GROUP):
        dst_ref[head * BLOCK_TOKENS:(head + 1) * BLOCK_TOKENS, :] = row_ref[
            0, which, :, head * HEAD_SIZE:(head + 1) * HEAD_SIZE
        ]


def causal_mask(offset):
    token = lax.broadcasted_iota(jnp.int32, (BLOCK_TOKENS, ROWS), 0)
    query = lax.broadcasted_iota(jnp.int32, (BLOCK_TOKENS, ROWS), 1)
    return token <= (query & (BLOCK_TOKENS - 1)) + BLOCK_TOKENS * offset


def block_offset(info_ref, plane, query_row):
    offset = SIDE * plane + query_row - info_ref[1]
    position = SIDE * info_ref[0] + query_row
    return offset, (offset >= 0) & (position - offset >= info_ref[2 + query_row])


def group_valid(info_ref, first, last, query_row):
    return [block_offset(info_ref, ORDER[slot], query_row) for slot in range(first, last)]


def masked(value, checks, first, fill):
    parts = []
    for index, (offset, valid) in enumerate(checks):
        part = value[index * BLOCK_TOKENS:(index + 1) * BLOCK_TOKENS]
        keep = valid if ORDER[first + index] else valid & causal_mask(offset)
        parts.append(jnp.where(keep, part, fill))
    return parts[0] if len(parts) == 1 else jnp.concatenate(parts, axis=0)


def products(kv_ref, first, last, qs, gs):
    rows = (last - first) * BLOCK_TOKENS
    key = kv_ref[first:last, :, :HEAD_SIZE].reshape(rows, HEAD_SIZE)
    value = kv_ref[first:last, :, HEAD_SIZE:].reshape(rows, HEAD_SIZE)
    score = lax.dot_general(key, qs, NT, preferred_element_type=jnp.float32)
    dprob = lax.dot_general(value, gs, NT, preferred_element_type=jnp.float32)
    return score, dprob


def stats_kernel(first_turn, info_ref, row_ref, kv_ref, *refs):
    out_ref, qs_ref, gs_ref, run_ref = refs[-4:]
    if first_turn:

        @pl.when(pl.program_id(0) == 0)
        def _():
            for target in range(SIDE):
                out_ref[target, info_ref[1]] = refs[0][0]

    query_row = (info_ref[1] - first_turn - pl.program_id(0)) & (SIDE - 1)
    stack_heads(row_ref, 0, qs_ref)
    stack_heads(row_ref, 1, gs_ref)
    run_ref[0:1, :] = jnp.full((1, ROWS), NEGATIVE, jnp.float32)
    run_ref[1:, :] = jnp.zeros((7, ROWS), jnp.float32)
    for first, last in EVEN_GROUPS + ODD_GROUPS:
        checks = group_valid(info_ref, first, last, query_row)

        @pl.when(functools.reduce(jnp.logical_or, [valid for _, valid in checks]))
        def _():
            score, dprob = products(kv_ref, first, last, qs_ref[...], gs_ref[...])
            score = masked(score, checks, first, NEGATIVE)
            old = run_ref[0:1, :]
            top = jnp.maximum(old, jnp.max(score, axis=0, keepdims=True))
            weight = jnp.exp2((score - top) * EXP_SCALE)
            keep = jnp.exp2((old - top) * EXP_SCALE)
            run_ref[0:1, :] = top
            run_ref[1:2, :] = run_ref[1:2, :] * keep + jnp.sum(weight, axis=0, keepdims=True)
            run_ref[2:3, :] = run_ref[2:3, :] * keep + jnp.sum(
                weight * dprob, axis=0, keepdims=True
            )

    total = run_ref[1:2, :]
    some = total > 0.0
    safe = jnp.where(some, total, 1.0)
    lse = jnp.where(some, run_ref[0:1, :] * EXP_SCALE + jnp.log2(safe), NEGATIVE)
    mean = run_ref[2:3, :] / safe
    if first_turn:
        for target in range(SIDE):
            out_ref[target, query_row, 0:1, :] = lse
            out_ref[target, query_row, 1:2, :] = mean
    else:
        out_ref[0, 0:1, :] = lse
        out_ref[0, 1:2, :] = mean


def grads_kernel(groups, info_ref, row_ref, kv_ref, stats_ref, out_ref, qs_ref, gs_ref, acc_ref):
    query_row = pl.program_id(0)
    base = groups[0][0]

    @pl.when(query_row == 0)
    def _():
        acc_ref[...] = jnp.zeros(acc_ref.shape, jnp.float32)

    stack_heads(row_ref, 0, qs_ref)
    stack_heads(row_ref, 1, gs_ref)
    parts = [stats_ref[source, 0, 0:1, :] for source in range(SIDE)]
    top = functools.reduce(jnp.maximum, parts)
    shares = [jnp.exp2(part - top) for part in parts]
    total = sum(shares)
    lse = top + jnp.log2(total)
    inner = sum(stats_ref[source, 0, 1:2, :] * shares[source] for source in range(SIDE))
    delta = inner / total
    for first, last in groups:
        checks = group_valid(info_ref, first, last, query_row)

        @pl.when(functools.reduce(jnp.logical_or, [valid for _, valid in checks]))
        def _():
            qs, gs = qs_ref[...], gs_ref[...]
            score, dprob = products(kv_ref, first, last, qs, gs)
            prob = masked(jnp.exp2(score * EXP_SCALE - lse), checks, first, 0.0)
            dscore = (prob * (dprob - delta)).astype(jnp.bfloat16)
            key_part = lax.dot_general(dscore, qs, NN, preferred_element_type=jnp.float32)
            value_part = lax.dot_general(
                prob.astype(jnp.bfloat16), gs, NN, preferred_element_type=jnp.float32
            )
            shape = (last - first, BLOCK_TOKENS, HEAD_SIZE)
            at = slice(first - base, last - base)
            acc_ref[at, :, :HEAD_SIZE] += (key_part * SCALE).reshape(shape)
            acc_ref[at, :, HEAD_SIZE:] += value_part.reshape(shape)

    @pl.when(query_row == SIDE - 1)
    def _():
        out_ref[...] = acc_ref[...].astype(out_ref.dtype)


STACKS = [
    pltpu.VMEM((ROWS, HEAD_SIZE), jnp.bfloat16),
    pltpu.VMEM((ROWS, HEAD_SIZE), jnp.bfloat16),
]
PARAMS = pltpu.CompilerParams(vmem_limit_bytes=40 * 1024 * 1024)
ROW_SHAPE = (1, 2, BLOCK_TOKENS, GROUP * HEAD_SIZE)
OWN_STATS = (1, STATS, ROWS)
ALL_STATS = (SIDE, SIDE, STATS, ROWS)


def whole(shape):
    return pl.BlockSpec(shape, lambda step, info: (0,) * len(shape))


def stats_pass(first_turn, info, rows, kv, *before):
    shape = ALL_STATS if first_turn else OWN_STATS

    def row_map(step, info):
        row = (info[1] - first_turn - step) & (SIDE - 1) if first_turn else 0
        return (row, 0, 0, 0)

    spec = pltpu.PrefetchScalarGridSpec(
        num_scalar_prefetch=1,
        grid=(SIDE - 1 if first_turn else 1,),
        in_specs=[pl.BlockSpec(ROW_SHAPE, row_map), whole(kv.shape)]
        + [whole(OWN_STATS) for _ in before],
        out_specs=whole(shape),
        scratch_shapes=STACKS + [pltpu.VMEM((8, ROWS), jnp.float32)],
    )
    return pl.pallas_call(
        functools.partial(stats_kernel, first_turn),
        out_shape=jax.ShapeDtypeStruct(shape, jnp.float32),
        grid_spec=spec,
        compiler_params=PARAMS,
        name="stats" + str(first_turn),
    )(info, rows, kv, *before)


def grads_pass(groups, dtype, info, rows, kv, stats):
    shape = (groups[-1][1] - groups[0][0], BLOCK_TOKENS, 2 * HEAD_SIZE)
    spec = pltpu.PrefetchScalarGridSpec(
        num_scalar_prefetch=1,
        grid=(SIDE,),
        in_specs=[
            pl.BlockSpec(ROW_SHAPE, lambda step, info: (step, 0, 0, 0)),
            whole(kv.shape),
            pl.BlockSpec((SIDE, 1, STATS, ROWS), lambda step, info: (0, step, 0, 0)),
        ],
        out_specs=whole(shape),
        scratch_shapes=STACKS + [pltpu.VMEM(shape, jnp.float32)],
    )
    return pl.pallas_call(
        functools.partial(grads_kernel, groups),
        out_shape=jax.ShapeDtypeStruct(shape, dtype),
        grid_spec=spec,
        compiler_params=PARAMS,
        name="grads" + str(groups[0][0]),
    )(info, rows, kv, stats)


def pick_kernel(pick_ref, left_ref, right_ref, out_ref):
    out_ref[0, :, :128] = left_ref[...]
    out_ref[0, :, 128:] = right_ref[...]


def pick_features(hidden, head):
    pick = jnp.stack([2 * (head % 2), head // 2]).astype(jnp.int32)

    def half_spec(half):
        return pl.BlockSpec(
            (BLOCK_TOKENS, 128), lambda lo, pick: (0, (pick[0] + half) * 16 + lo * 4 + pick[1])
        )

    spec = pltpu.PrefetchScalarGridSpec(
        num_scalar_prefetch=1,
        grid=(SIDE,),
        in_specs=[half_spec(0), half_spec(1)],
        out_specs=pl.BlockSpec((1, BLOCK_TOKENS, 256), lambda lo, pick: (lo, 0, 0)),
    )
    return pl.pallas_call(
        pick_kernel,
        out_shape=jax.ShapeDtypeStruct((SIDE, BLOCK_TOKENS, 256), hidden.dtype),
        grid_spec=spec,
        name="pick",
    )(pick, hidden, hidden)


def square_kernel(parts_ref, weight_ref, spread_ref):
    weight = sum(parts_ref[source].astype(jnp.float32) for source in range(SIDE))
    weight_ref[...] = weight
    squares = jnp.sum((weight * weight).reshape(16, 8, 256), axis=0)
    squares = squares[:, :128] + squares[:, 128:]
    spread_ref[...] = jnp.broadcast_to(squares, spread_ref.shape)


def square_pass(parts):
    return pl.pallas_call(
        square_kernel,
        out_shape=(
            jax.ShapeDtypeStruct((BLOCK_TOKENS, 256), jnp.float32),
            jax.ShapeDtypeStruct((32, 8, 128), jnp.float32),
        ),
        name="square",
    )(parts)


def spread_kernel(parts_ref, out_ref):
    out_ref[...] = jnp.broadcast_to(jnp.sum(parts_ref[...], axis=0), out_ref.shape)


def spread_pass(parts):
    return pl.pallas_call(
        spread_kernel, out_shape=jax.ShapeDtypeStruct((16, 8, 128), jnp.float32), name="spread"
    )(parts)


def finish_kernel(parts_ref, weight_ref, key_ref, value_ref):
    total = jnp.sum(jnp.sum(parts_ref[...], axis=0))
    mean_square = total / (2.0 * MODEL_WIDTH * KEY_VALUE_HEADS * HEAD_SIZE)
    factor = 1.0 / jnp.sqrt(jnp.full((1, HEAD_SIZE), mean_square + 1e-06, jnp.float32))
    key_ref[...] = weight_ref[:, :HEAD_SIZE] * factor
    value_ref[...] = weight_ref[:, HEAD_SIZE:] * factor


def finish_pass(parts, weight):
    shape = jax.ShapeDtypeStruct((BLOCK_TOKENS, HEAD_SIZE), jnp.float32)
    return pl.pallas_call(finish_kernel, out_shape=(shape, shape), name="finish")(parts, weight)


def rotary_tables(positions):
    half = HEAD_SIZE // 2
    freqs = 500000.0 ** (-(jnp.arange(half, dtype=jnp.float32) * 2.0) / HEAD_SIZE)
    angles = positions.astype(jnp.float32)[:, None] * freqs[None, :]
    cosine, sine = jnp.cos(angles), jnp.sin(angles)
    return jnp.concatenate([cosine, cosine], -1), jnp.concatenate([sine, sine], -1)


def exchange(value, axis):
    return lax.all_to_all(value, axis, split_axis=0, concat_axis=0, tiled=True)


def per_device(hidden, queries, keys, values, output_gradient, doc_blocks):
    z = lax.axis_index(Z)
    row = lax.axis_index("y")
    head = lax.axis_index("head")
    ends = jnp.cumsum(doc_blocks)
    rows = SIDE * z + jnp.arange(SIDE)
    firsts = jnp.max(jnp.where(ends[None, :] <= rows[:, None], ends[None, :], 0), axis=1)
    info = jnp.concatenate([jnp.stack([z, row]), firsts]).astype(jnp.int32)
    here = SIDE * z + row
    f32 = jnp.float32

    own = jnp.concatenate([keys, values], axis=1)[None]
    four = rotate(own, Z, 4)
    own_row = jnp.stack([queries, output_gradient])
    query_rows = lax.all_gather(own_row, "y")
    query_rows = pltpu.with_memory_space_constraint(query_rows, pltpu.HBM)
    even = jnp.concatenate([own, four])
    two = rotate(even, Z, 2)
    odd = rotate(jnp.concatenate([own, two[0:1], four]), Z, 1)
    column = jnp.concatenate([own, two[0:1], four, two[1:2], odd])

    stats = stats_pass(0, info, own_row[None], column)
    picked = pick_features(hidden, head)
    picked, _ = lax.optimization_barrier((picked, odd))
    tokens = exchange(picked, "z_lo")
    stats = stats_pass(1, info, query_rows, column, stats)
    tokens, stats = lax.optimization_barrier((tokens, stats))
    features = lax.all_gather(tokens.reshape(SIDE * BLOCK_TOKENS, 256), "head", axis=0)

    stats = exchange(stats, "y")
    odd_grads = grads_pass(ODD_GROUPS, jnp.bfloat16, info, query_rows, column, stats)
    odd_back = rotate(odd_grads, Z, -1)
    even_grads = grads_pass(EVEN_GROUPS, f32, info, query_rows, column, stats)
    odd_back = odd_back.astype(f32)
    s0 = even_grads[0] + odd_back[0]
    s2 = even_grads[1] + odd_back[1]
    s4 = even_grads[2] + odd_back[2]
    two_back = rotate(jnp.stack([s2, even_grads[3]]).astype(jnp.bfloat16), Z, -2).astype(f32)
    s0 = s0 + two_back[0]
    s4 = s4 + two_back[1]
    four_back = rotate(s4.astype(jnp.bfloat16), Z, -4).astype(f32)
    s0 = s0 + four_back

    cosine, sine = rotary_tables(here * BLOCK_TOKENS + jnp.arange(BLOCK_TOKENS))
    key_grad = s0[:, :HEAD_SIZE]
    half = HEAD_SIZE // 2
    turned = jnp.concatenate([-key_grad[:, half:], key_grad[:, :half]], axis=-1)
    pre = jnp.concatenate([key_grad * cosine - turned * sine, s0[:, HEAD_SIZE:]], axis=1)
    pre = pre.astype(jnp.bfloat16)
    gathered = exchange(jnp.broadcast_to(pre, (SIDE,) + pre.shape), "z_lo")
    gathered = gathered.reshape(SIDE * BLOCK_TOKENS, 2 * HEAD_SIZE)

    weight = lax.dot_general(
        features, gathered, (((1,), (0,)), ((), ())), preferred_element_type=f32
    ).astype(jnp.bfloat16)
    weight = exchange(weight.reshape(SIDE, SIDE * BLOCK_TOKENS, 256), "y")
    weight = jnp.sum(weight.astype(f32), axis=0).astype(jnp.bfloat16)
    weight = exchange(weight.reshape(SIDE, BLOCK_TOKENS, 256), "z_hi")
    weight, spread = square_pass(weight)
    spread = spread_pass(exchange(spread, ("y", "head")))
    return finish_pass(exchange(spread, Z), weight)


def solution(mesh):
    devices = mesh.devices.reshape(4, 4, 4, 8)
    split = Mesh(devices, ("z_hi", "z_lo", "y", "head"))
    placed = (P(CTX, None),) + (P(CTX, "head"),) * 4 + (P(),)
    return jax.shard_map(
        per_device,
        mesh=split,
        in_specs=placed,
        out_specs=(P(CTX, "head"), P(CTX, "head")),
        check_vma=False,
    )
```

```python
import functools

import jax
import jax.numpy as jnp
from jax import lax
from jax.experimental import pallas as pl
from jax.experimental.pallas import tpu as pltpu
from jax.sharding import Mesh, PartitionSpec as P

MODEL_WIDTH = 8192
QUERY_HEADS = 64
KEY_VALUE_HEADS = 8
HEAD_SIZE = 128
BLOCK_TOKENS = 128
GROUP = QUERY_HEADS // KEY_VALUE_HEADS
ROWS = GROUP * BLOCK_TOKENS
PLANES = 7
SIDE = 4
STATS = 2
ORDER = (0, 2, 4, 6, 1, 3, 5)
EVEN_GROUPS = ((0, 4),)
ODD_GROUPS = ((4, 7),)
NEGATIVE = -1e30
SCALE = HEAD_SIZE ** (-0.5)
LOG2E = 1.4426950408889634
EXP_SCALE = SCALE * LOG2E
Z = ("z_hi", "z_lo")
CTX = ("z_hi", "z_lo", "y")

NT = (((1,), (1,)), ((), ()))
NN = (((1,), (0,)), ((), ()))
TN = (((0,), (0,)), ((), ()))


def axis_total(axis):
    names = axis if isinstance(axis, tuple) else (axis,)
    total = 1
    for name in names:
        total *= lax.axis_size(name)
    return total


def rotate(value, axis, steps):
    count = axis_total(axis)
    return lax.ppermute(value, axis, [(at, (at + steps) % count) for at in range(count)])


def stack_heads(src_ref, dst_ref):
    for head in range(GROUP):
        dst_ref[head * BLOCK_TOKENS:(head + 1) * BLOCK_TOKENS, :] = src_ref[
            :, head * HEAD_SIZE:(head + 1) * HEAD_SIZE
        ]


def causal_mask(offset):
    token = lax.broadcasted_iota(jnp.int32, (BLOCK_TOKENS, ROWS), 0)
    query = lax.broadcasted_iota(jnp.int32, (BLOCK_TOKENS, ROWS), 1)
    return token <= (query & (BLOCK_TOKENS - 1)) + BLOCK_TOKENS * offset


def block_offset(info_ref, plane, query_row):
    offset = SIDE * plane + query_row - info_ref[1]
    position = SIDE * info_ref[0] + query_row
    return offset, (offset >= 0) & (position - offset >= info_ref[2 + query_row])


def group_valid(info_ref, first, last, query_row):
    return [block_offset(info_ref, ORDER[slot], query_row) for slot in range(first, last)]


def masked(value, checks, first, fill):
    parts = []
    for index, (offset, valid) in enumerate(checks):
        part = value[index * BLOCK_TOKENS:(index + 1) * BLOCK_TOKENS]
        keep = valid if ORDER[first + index] else valid & causal_mask(offset)
        parts.append(jnp.where(keep, part, fill))
    return parts[0] if len(parts) == 1 else jnp.concatenate(parts, axis=0)


def products(kv_ref, first, last, qs, gs):
    rows = (last - first) * BLOCK_TOKENS
    key = kv_ref[first:last, :, :HEAD_SIZE].reshape(rows, HEAD_SIZE)
    value = kv_ref[first:last, :, HEAD_SIZE:].reshape(rows, HEAD_SIZE)
    score = lax.dot_general(key, qs, NT, preferred_element_type=jnp.float32)
    dprob = lax.dot_general(value, gs, NT, preferred_element_type=jnp.float32)
    return score, dprob


def stats_kernel(first_turn, info_ref, *refs):
    out_ref, qs_ref, gs_ref, run_ref = refs[-4:]
    if first_turn:
        row_ref, kv_ref, own_ref = refs[:3]
        pair = row_ref.at[0, 0], row_ref.at[0, 1]

        @pl.when(pl.program_id(0) == 0)
        def _():
            for target in range(SIDE):
                out_ref[target, info_ref[1]] = own_ref[0]

    else:
        kv_ref = refs[2]
        pair = refs[:2]
    query_row = (info_ref[1] - first_turn - pl.program_id(0)) & (SIDE - 1)
    stack_heads(pair[0], qs_ref)
    stack_heads(pair[1], gs_ref)
    run_ref[0:1, :] = jnp.full((1, ROWS), NEGATIVE, jnp.float32)
    run_ref[1:, :] = jnp.zeros((7, ROWS), jnp.float32)
    for first, last in EVEN_GROUPS + ODD_GROUPS:
        checks = group_valid(info_ref, first, last, query_row)

        @pl.when(functools.reduce(jnp.logical_or, [valid for _, valid in checks]))
        def _():
            score, dprob = products(kv_ref, first, last, qs_ref[...], gs_ref[...])
            score = masked(score, checks, first, NEGATIVE)
            old = run_ref[0:1, :]
            top = jnp.maximum(old, jnp.max(score, axis=0, keepdims=True))
            weight = jnp.exp2((score - top) * EXP_SCALE)
            keep = jnp.exp2((old - top) * EXP_SCALE)
            run_ref[0:1, :] = top
            run_ref[1:2, :] = run_ref[1:2, :] * keep + jnp.sum(weight, axis=0, keepdims=True)
            run_ref[2:3, :] = run_ref[2:3, :] * keep + jnp.sum(
                weight * dprob, axis=0, keepdims=True
            )

    total = run_ref[1:2, :]
    some = total > 0.0
    safe = jnp.where(some, total, 1.0)
    lse = jnp.where(some, run_ref[0:1, :] * EXP_SCALE + jnp.log2(safe), NEGATIVE)
    mean = run_ref[2:3, :] / safe
    if first_turn:
        for target in range(SIDE):
            out_ref[target, query_row, 0:1, :] = lse
            out_ref[target, query_row, 1:2, :] = mean
    else:
        out_ref[0, 0:1, :] = lse
        out_ref[0, 1:2, :] = mean


def grads_kernel(groups, info_ref, row_ref, kv_ref, stats_ref, out_ref, qs_ref, gs_ref, acc_ref):
    query_row = pl.program_id(0)
    base = groups[0][0]

    @pl.when(query_row == 0)
    def _():
        acc_ref[...] = jnp.zeros(acc_ref.shape, jnp.float32)

    stack_heads(row_ref.at[0, 0], qs_ref)
    stack_heads(row_ref.at[0, 1], gs_ref)
    parts = [stats_ref[source, 0, 0:1, :] for source in range(SIDE)]
    top = functools.reduce(jnp.maximum, parts)
    shares = [jnp.exp2(part - top) for part in parts]
    total = sum(shares)
    lse = top + jnp.log2(total)
    inner = sum(stats_ref[source, 0, 1:2, :] * shares[source] for source in range(SIDE))
    delta = inner / total
    for first, last in groups:
        checks = group_valid(info_ref, first, last, query_row)

        @pl.when(functools.reduce(jnp.logical_or, [valid for _, valid in checks]))
        def _():
            qs, gs = qs_ref[...], gs_ref[...]
            score, dprob = products(kv_ref, first, last, qs, gs)
            prob = masked(jnp.exp2(score * EXP_SCALE - lse), checks, first, 0.0)
            dscore = (prob * (dprob - delta)).astype(jnp.bfloat16)
            key_part = lax.dot_general(dscore, qs, NN, preferred_element_type=jnp.float32)
            value_part = lax.dot_general(
                prob.astype(jnp.bfloat16), gs, NN, preferred_element_type=jnp.float32
            )
            shape = (last - first, BLOCK_TOKENS, HEAD_SIZE)
            at = slice(first - base, last - base)
            acc_ref[at, :, :HEAD_SIZE] += (key_part * SCALE).reshape(shape)
            acc_ref[at, :, HEAD_SIZE:] += value_part.reshape(shape)

    @pl.when(query_row == SIDE - 1)
    def _():
        out_ref[...] = acc_ref[...].astype(out_ref.dtype)


STACKS = [
    pltpu.VMEM((ROWS, HEAD_SIZE), jnp.bfloat16),
    pltpu.VMEM((ROWS, HEAD_SIZE), jnp.bfloat16),
]
PARAMS = pltpu.CompilerParams(vmem_limit_bytes=40 * 1024 * 1024)
SMALL = pltpu.CompilerParams(vmem_limit_bytes=8 * 1024 * 1024)
ROW_SHAPE = (1, 2, BLOCK_TOKENS, GROUP * HEAD_SIZE)
OWN_STATS = (1, STATS, ROWS)
ALL_STATS = (SIDE, SIDE, STATS, ROWS)


def whole(shape):
    return pl.BlockSpec(shape, lambda step, info: (0,) * len(shape))


def stats_pass(first_turn, info, *arrays):
    shape = ALL_STATS if first_turn else OWN_STATS
    specs = [whole(array.shape) for array in arrays]
    if first_turn:
        specs[0] = pl.BlockSpec(
            ROW_SHAPE, lambda step, info: ((info[1] - first_turn - step) & (SIDE - 1), 0, 0, 0)
        )
    spec = pltpu.PrefetchScalarGridSpec(
        num_scalar_prefetch=1,
        grid=(SIDE - 1 if first_turn else 1,),
        in_specs=specs,
        out_specs=whole(shape),
        scratch_shapes=STACKS + [pltpu.VMEM((8, ROWS), jnp.float32)],
    )
    return pl.pallas_call(
        functools.partial(stats_kernel, first_turn),
        out_shape=jax.ShapeDtypeStruct(shape, jnp.float32),
        grid_spec=spec,
        compiler_params=PARAMS,
        name="stats" + str(first_turn),
    )(info, *arrays)


def grads_pass(groups, dtype, info, rows, kv, stats):
    shape = (groups[-1][1] - groups[0][0], BLOCK_TOKENS, 2 * HEAD_SIZE)
    spec = pltpu.PrefetchScalarGridSpec(
        num_scalar_prefetch=1,
        grid=(SIDE,),
        in_specs=[
            pl.BlockSpec(ROW_SHAPE, lambda step, info: (step, 0, 0, 0)),
            whole(kv.shape),
            pl.BlockSpec((SIDE, 1, STATS, ROWS), lambda step, info: (0, step, 0, 0)),
        ],
        out_specs=whole(shape),
        scratch_shapes=STACKS + [pltpu.VMEM(shape, jnp.float32)],
    )
    return pl.pallas_call(
        functools.partial(grads_kernel, groups),
        out_shape=jax.ShapeDtypeStruct(shape, dtype),
        grid_spec=spec,
        compiler_params=PARAMS,
        name="grads" + str(groups[0][0]),
    )(info, rows, kv, stats)


def pick_kernel(pick_ref, left_ref, right_ref, out_ref):
    out_ref[0, :, :128] = left_ref[...]
    out_ref[0, :, 128:] = right_ref[...]


def pick_features(hidden, head):
    pick = jnp.stack([2 * (head % 2), head // 2]).astype(jnp.int32)

    def half_spec(half):
        return pl.BlockSpec(
            (BLOCK_TOKENS, 128), lambda lo, pick: (0, (pick[0] + half) * 16 + lo * 4 + pick[1])
        )

    spec = pltpu.PrefetchScalarGridSpec(
        num_scalar_prefetch=1,
        grid=(SIDE,),
        in_specs=[half_spec(0), half_spec(1)],
        out_specs=pl.BlockSpec((1, BLOCK_TOKENS, 256), lambda lo, pick: (lo, 0, 0)),
    )
    return pl.pallas_call(
        pick_kernel,
        out_shape=jax.ShapeDtypeStruct((SIDE, BLOCK_TOKENS, 256), hidden.dtype),
        grid_spec=spec,
        compiler_params=SMALL,
        name="pick",
    )(pick, hidden, hidden)


VMEM_SPEC = pl.BlockSpec(memory_space=pltpu.VMEM)


def square_kernel(parts_ref, weight_ref, spread_ref):
    weight = sum(parts_ref[source].astype(jnp.float32) for source in range(SIDE))
    weight_ref[...] = weight
    squares = jnp.sum((weight * weight).reshape(16, 8, 256), axis=0)
    squares = squares[:, :128] + squares[:, 128:]
    spread_ref[...] = jnp.broadcast_to(squares, spread_ref.shape)


def square_pass(parts):
    return pl.pallas_call(
        square_kernel,
        out_shape=(
            jax.ShapeDtypeStruct((BLOCK_TOKENS, 256), jnp.float32),
            jax.ShapeDtypeStruct((32, 8, 128), jnp.float32),
        ),
        in_specs=[VMEM_SPEC],
        out_specs=(VMEM_SPEC, VMEM_SPEC),
        compiler_params=SMALL,
        name="square",
    )(parts)


def spread_kernel(parts_ref, out_ref):
    out_ref[...] = jnp.broadcast_to(jnp.sum(parts_ref[...], axis=0), out_ref.shape)


def spread_pass(parts):
    return pl.pallas_call(
        spread_kernel,
        out_shape=jax.ShapeDtypeStruct((16, 8, 128), jnp.float32),
        in_specs=[VMEM_SPEC],
        out_specs=VMEM_SPEC,
        compiler_params=SMALL,
        name="spread",
    )(parts)


def finish_kernel(parts_ref, weight_ref, key_ref, value_ref):
    total = jnp.sum(jnp.sum(parts_ref[...], axis=0))
    mean_square = total / (2.0 * MODEL_WIDTH * KEY_VALUE_HEADS * HEAD_SIZE)
    factor = 1.0 / jnp.sqrt(jnp.full((1, HEAD_SIZE), mean_square + 1e-06, jnp.float32))
    key_ref[...] = weight_ref[:, :HEAD_SIZE] * factor
    value_ref[...] = weight_ref[:, HEAD_SIZE:] * factor


def finish_pass(parts, weight):
    shape = jax.ShapeDtypeStruct((BLOCK_TOKENS, HEAD_SIZE), jnp.float32)
    return pl.pallas_call(
        finish_kernel,
        out_shape=(shape, shape),
        in_specs=[VMEM_SPEC, VMEM_SPEC],
        out_specs=(VMEM_SPEC, VMEM_SPEC),
        compiler_params=SMALL,
        name="finish",
    )(parts, weight)


def rotary_tables(positions):
    half = HEAD_SIZE // 2
    freqs = 500000.0 ** (-(jnp.arange(half, dtype=jnp.float32) * 2.0) / HEAD_SIZE)
    angles = positions.astype(jnp.float32)[:, None] * freqs[None, :]
    cosine, sine = jnp.cos(angles), jnp.sin(angles)
    return jnp.concatenate([cosine, cosine], -1), jnp.concatenate([sine, sine], -1)


def exchange(value, axis):
    return lax.all_to_all(value, axis, split_axis=0, concat_axis=0, tiled=True)


def per_device(hidden, queries, keys, values, output_gradient, doc_blocks):
    z = lax.axis_index(Z)
    row = lax.axis_index("y")
    head = lax.axis_index("head")
    ends = jnp.cumsum(doc_blocks)
    rows = SIDE * z + jnp.arange(SIDE)
    firsts = jnp.max(jnp.where(ends[None, :] <= rows[:, None], ends[None, :], 0), axis=1)
    info = jnp.concatenate([jnp.stack([z, row]), firsts]).astype(jnp.int32)
    here = SIDE * z + row
    f32 = jnp.float32

    own = jnp.concatenate([keys, values], axis=1)[None]
    four = rotate(own, Z, 4)
    own_row = jnp.stack([queries, output_gradient])
    query_rows = lax.all_gather(own_row, "y")
    query_rows = pltpu.with_memory_space_constraint(query_rows, pltpu.HBM)
    even = jnp.concatenate([own, four])
    two = rotate(even, Z, 2)
    odd = rotate(jnp.concatenate([own, two[0:1], four]), Z, 1)
    column = jnp.concatenate([own, two[0:1], four, two[1:2], odd])

    stats = stats_pass(0, info, queries, output_gradient, column)
    picked = pick_features(hidden, head)
    picked, _ = lax.optimization_barrier((picked, odd))
    tokens = exchange(picked, "z_lo")
    stats = stats_pass(1, info, query_rows, column, stats)
    tokens, stats = lax.optimization_barrier((tokens, stats))
    features = lax.all_gather(tokens.reshape(SIDE * BLOCK_TOKENS, 256), "head", axis=0)

    stats = exchange(stats, "y")
    odd_grads = grads_pass(ODD_GROUPS, jnp.bfloat16, info, query_rows, column, stats)
    odd_back = rotate(odd_grads, Z, -1)
    even_grads = grads_pass(EVEN_GROUPS, f32, info, query_rows, column, stats)
    odd_back = odd_back.astype(f32)
    s0 = even_grads[0] + odd_back[0]
    s2 = even_grads[1] + odd_back[1]
    s4 = even_grads[2] + odd_back[2]
    two_back = rotate(jnp.stack([s2, even_grads[3]]).astype(jnp.bfloat16), Z, -2).astype(f32)
    s0 = s0 + two_back[0]
    s4 = s4 + two_back[1]
    four_back = rotate(s4.astype(jnp.bfloat16), Z, -4).astype(f32)
    s0 = s0 + four_back

    cosine, sine = rotary_tables(here * BLOCK_TOKENS + jnp.arange(BLOCK_TOKENS))
    key_grad = s0[:, :HEAD_SIZE]
    half = HEAD_SIZE // 2
    turned = jnp.concatenate([-key_grad[:, half:], key_grad[:, :half]], axis=-1)
    pre = jnp.concatenate([key_grad * cosine - turned * sine, s0[:, HEAD_SIZE:]], axis=1)
    pre = pre.astype(jnp.bfloat16)
    gathered = exchange(jnp.broadcast_to(pre, (SIDE,) + pre.shape), "z_lo")
    gathered = gathered.reshape(SIDE * BLOCK_TOKENS, 2 * HEAD_SIZE)

    weight = lax.dot_general(
        features, gathered, (((1,), (0,)), ((), ())), preferred_element_type=f32
    ).astype(jnp.bfloat16)
    weight = exchange(weight.reshape(SIDE, SIDE * BLOCK_TOKENS, 256), "y")
    weight = jnp.sum(weight.astype(f32), axis=0).astype(jnp.bfloat16)
    weight = exchange(weight.reshape(SIDE, BLOCK_TOKENS, 256), "z_hi")
    weight, spread = square_pass(weight)
    spread = spread_pass(exchange(spread, ("y", "head")))
    return finish_pass(exchange(spread, Z), weight)


def solution(mesh):
    devices = mesh.devices.reshape(4, 4, 4, 8)
    split = Mesh(devices, ("z_hi", "z_lo", "y", "head"))
    placed = (P(CTX, None),) + (P(CTX, "head"),) * 4 + (P(),)
    return jax.shard_map(
        per_device,
        mesh=split,
        in_specs=placed,
        out_specs=(P(CTX, "head"), P(CTX, "head")),
        check_vma=False,
    )
```

```python
import functools

import jax
import jax.numpy as jnp
from jax import lax
from jax.experimental import pallas as pl
from jax.experimental.pallas import tpu as pltpu
from jax.sharding import Mesh, PartitionSpec as P

MODEL_WIDTH = 8192
QUERY_HEADS = 64
KEY_VALUE_HEADS = 8
HEAD_SIZE = 128
BLOCK_TOKENS = 128
GROUP = QUERY_HEADS // KEY_VALUE_HEADS
ROWS = GROUP * BLOCK_TOKENS
PLANES = 7
SIDE = 4
STATS = 2
ORDER = (0, 2, 4, 6, 1, 3, 5)
EVEN_GROUPS = ((0, 4),)
ODD_GROUPS = ((4, 7),)
NEGATIVE = -1e30
SCALE = HEAD_SIZE ** (-0.5)
LOG2E = 1.4426950408889634
EXP_SCALE = SCALE * LOG2E
Z = ("z_hi", "z_lo")
CTX = ("z_hi", "z_lo", "y")

NT = (((1,), (1,)), ((), ()))
NN = (((1,), (0,)), ((), ()))
TN = (((0,), (0,)), ((), ()))


def axis_total(axis):
    names = axis if isinstance(axis, tuple) else (axis,)
    total = 1
    for name in names:
        total *= lax.axis_size(name)
    return total


def rotate(value, axis, steps):
    count = axis_total(axis)
    return lax.ppermute(value, axis, [(at, (at + steps) % count) for at in range(count)])


def stack_heads(row_ref, which, dst_ref):
    for head in range(GROUP):
        dst_ref[head * BLOCK_TOKENS:(head + 1) * BLOCK_TOKENS, :] = row_ref[
            0, which, :, head * HEAD_SIZE:(head + 1) * HEAD_SIZE
        ]


def causal_mask(offset):
    token = lax.broadcasted_iota(jnp.int32, (BLOCK_TOKENS, ROWS), 0)
    query = lax.broadcasted_iota(jnp.int32, (BLOCK_TOKENS, ROWS), 1)
    return token <= (query & (BLOCK_TOKENS - 1)) + BLOCK_TOKENS * offset


def block_offset(info_ref, plane, query_row):
    offset = SIDE * plane + query_row - info_ref[1]
    position = SIDE * info_ref[0] + query_row
    return offset, (offset >= 0) & (position - offset >= info_ref[2 + query_row])


def group_valid(info_ref, first, last, query_row):
    return [block_offset(info_ref, ORDER[slot], query_row) for slot in range(first, last)]


def masked(value, checks, first, fill):
    parts = []
    for index, (offset, valid) in enumerate(checks):
        part = value[index * BLOCK_TOKENS:(index + 1) * BLOCK_TOKENS]
        keep = valid if ORDER[first + index] else valid & causal_mask(offset)
        parts.append(jnp.where(keep, part, fill))
    return parts[0] if len(parts) == 1 else jnp.concatenate(parts, axis=0)


def products(kv_ref, first, last, qs, gs):
    rows = (last - first) * BLOCK_TOKENS
    key = kv_ref[first:last, :, :HEAD_SIZE].reshape(rows, HEAD_SIZE)
    value = kv_ref[first:last, :, HEAD_SIZE:].reshape(rows, HEAD_SIZE)
    score = lax.dot_general(key, qs, NT, preferred_element_type=jnp.float32)
    dprob = lax.dot_general(value, gs, NT, preferred_element_type=jnp.float32)
    return score, dprob


def stats_kernel(info_ref, row_ref, kv_ref, out_ref, qs_ref, gs_ref, run_ref):
    query_row = pl.program_id(0)
    stack_heads(row_ref, 0, qs_ref)
    stack_heads(row_ref, 1, gs_ref)
    run_ref[0:1, :] = jnp.full((1, ROWS), NEGATIVE, jnp.float32)
    run_ref[1:, :] = jnp.zeros((7, ROWS), jnp.float32)
    for first, last in EVEN_GROUPS + ODD_GROUPS:
        checks = group_valid(info_ref, first, last, query_row)

        @pl.when(functools.reduce(jnp.logical_or, [valid for _, valid in checks]))
        def _():
            score, dprob = products(kv_ref, first, last, qs_ref[...], gs_ref[...])
            score = masked(score, checks, first, NEGATIVE)
            old = run_ref[0:1, :]
            top = jnp.maximum(old, jnp.max(score, axis=0, keepdims=True))
            weight = jnp.exp2((score - top) * EXP_SCALE)
            keep = jnp.exp2((old - top) * EXP_SCALE)
            run_ref[0:1, :] = top
            run_ref[1:2, :] = run_ref[1:2, :] * keep + jnp.sum(weight, axis=0, keepdims=True)
            run_ref[2:3, :] = run_ref[2:3, :] * keep + jnp.sum(
                weight * dprob, axis=0, keepdims=True
            )

    total = run_ref[1:2, :]
    some = total > 0.0
    safe = jnp.where(some, total, 1.0)
    lse = jnp.where(some, run_ref[0:1, :] * EXP_SCALE + jnp.log2(safe), NEGATIVE)
    mean = run_ref[2:3, :] / safe
    for target in range(SIDE):
        out_ref[target, 0, 0:1, :] = lse
        out_ref[target, 0, 1:2, :] = mean


def grads_kernel(groups, info_ref, row_ref, kv_ref, stats_ref, out_ref, qs_ref, gs_ref, acc_ref):
    query_row = pl.program_id(0)
    base = groups[0][0]

    @pl.when(query_row == 0)
    def _():
        acc_ref[...] = jnp.zeros(acc_ref.shape, jnp.float32)

    stack_heads(row_ref, 0, qs_ref)
    stack_heads(row_ref, 1, gs_ref)
    parts = [stats_ref[source, 0, 0:1, :] for source in range(SIDE)]
    top = functools.reduce(jnp.maximum, parts)
    shares = [jnp.exp2(part - top) for part in parts]
    total = sum(shares)
    lse = top + jnp.log2(total)
    inner = sum(stats_ref[source, 0, 1:2, :] * shares[source] for source in range(SIDE))
    delta = inner / total
    for first, last in groups:
        checks = group_valid(info_ref, first, last, query_row)

        @pl.when(functools.reduce(jnp.logical_or, [valid for _, valid in checks]))
        def _():
            qs, gs = qs_ref[...], gs_ref[...]
            score, dprob = products(kv_ref, first, last, qs, gs)
            prob = masked(jnp.exp2(score * EXP_SCALE - lse), checks, first, 0.0)
            dscore = (prob * (dprob - delta)).astype(jnp.bfloat16)
            key_part = lax.dot_general(dscore, qs, NN, preferred_element_type=jnp.float32)
            value_part = lax.dot_general(
                prob.astype(jnp.bfloat16), gs, NN, preferred_element_type=jnp.float32
            )
            shape = (last - first, BLOCK_TOKENS, HEAD_SIZE)
            at = slice(first - base, last - base)
            acc_ref[at, :, :HEAD_SIZE] += (key_part * SCALE).reshape(shape)
            acc_ref[at, :, HEAD_SIZE:] += value_part.reshape(shape)

    @pl.when(query_row == SIDE - 1)
    def _():
        out_ref[...] = acc_ref[...].astype(out_ref.dtype)


STACKS = [
    pltpu.VMEM((ROWS, HEAD_SIZE), jnp.bfloat16),
    pltpu.VMEM((ROWS, HEAD_SIZE), jnp.bfloat16),
]
PARAMS = pltpu.CompilerParams(vmem_limit_bytes=40 * 1024 * 1024)
SMALL = pltpu.CompilerParams(vmem_limit_bytes=8 * 1024 * 1024)
ROW_SHAPE = (1, 2, BLOCK_TOKENS, GROUP * HEAD_SIZE)
ROW_SPEC = pl.BlockSpec(ROW_SHAPE, lambda step, info: (step, 0, 0, 0))
STATS_SPEC = pl.BlockSpec((SIDE, 1, STATS, ROWS), lambda step, info: (0, step, 0, 0))


def whole(shape):
    return pl.BlockSpec(shape, lambda step, info: (0,) * len(shape))


def stats_pass(info, rows, kv):
    spec = pltpu.PrefetchScalarGridSpec(
        num_scalar_prefetch=1,
        grid=(SIDE,),
        in_specs=[ROW_SPEC, whole(kv.shape)],
        out_specs=STATS_SPEC,
        scratch_shapes=STACKS + [pltpu.VMEM((8, ROWS), jnp.float32)],
    )
    return pl.pallas_call(
        stats_kernel,
        out_shape=jax.ShapeDtypeStruct((SIDE, SIDE, STATS, ROWS), jnp.float32),
        grid_spec=spec,
        compiler_params=PARAMS,
        name="stats",
    )(info, rows, kv)


def grads_pass(groups, dtype, info, rows, kv, stats):
    shape = (groups[-1][1] - groups[0][0], BLOCK_TOKENS, 2 * HEAD_SIZE)
    spec = pltpu.PrefetchScalarGridSpec(
        num_scalar_prefetch=1,
        grid=(SIDE,),
        in_specs=[ROW_SPEC, whole(kv.shape), STATS_SPEC],
        out_specs=whole(shape),
        scratch_shapes=STACKS + [pltpu.VMEM(shape, jnp.float32)],
    )
    return pl.pallas_call(
        functools.partial(grads_kernel, groups),
        out_shape=jax.ShapeDtypeStruct(shape, dtype),
        grid_spec=spec,
        compiler_params=PARAMS,
        name="grads" + str(groups[0][0]),
    )(info, rows, kv, stats)


def pick_kernel(pick_ref, left_ref, right_ref, out_ref):
    out_ref[0, :, :128] = left_ref[...]
    out_ref[0, :, 128:] = right_ref[...]


def pick_features(hidden, head):
    pick = jnp.stack([2 * (head % 2), head // 2]).astype(jnp.int32)

    def half_spec(half):
        return pl.BlockSpec(
            (BLOCK_TOKENS, 128), lambda lo, pick: (0, (pick[0] + half) * 16 + lo * 4 + pick[1])
        )

    spec = pltpu.PrefetchScalarGridSpec(
        num_scalar_prefetch=1,
        grid=(SIDE,),
        in_specs=[half_spec(0), half_spec(1)],
        out_specs=pl.BlockSpec((1, BLOCK_TOKENS, 256), lambda lo, pick: (lo, 0, 0)),
    )
    return pl.pallas_call(
        pick_kernel,
        out_shape=jax.ShapeDtypeStruct((SIDE, BLOCK_TOKENS, 256), hidden.dtype),
        grid_spec=spec,
        compiler_params=SMALL,
        name="pick",
    )(pick, hidden, hidden)


VMEM_SPEC = pl.BlockSpec(memory_space=pltpu.VMEM)


def square_kernel(parts_ref, weight_ref, spread_ref):
    weight = sum(parts_ref[source].astype(jnp.float32) for source in range(SIDE))
    weight_ref[...] = weight
    squares = jnp.sum((weight * weight).reshape(16, 8, 256), axis=0)
    squares = squares[:, :128] + squares[:, 128:]
    spread_ref[...] = jnp.broadcast_to(squares, spread_ref.shape)


def square_pass(parts):
    return pl.pallas_call(
        square_kernel,
        out_shape=(
            jax.ShapeDtypeStruct((BLOCK_TOKENS, 256), jnp.float32),
            jax.ShapeDtypeStruct((32, 8, 128), jnp.float32),
        ),
        in_specs=[VMEM_SPEC],
        out_specs=(VMEM_SPEC, VMEM_SPEC),
        compiler_params=SMALL,
        name="square",
    )(parts)


def spread_kernel(parts_ref, out_ref):
    out_ref[...] = jnp.broadcast_to(jnp.sum(parts_ref[...], axis=0), out_ref.shape)


def spread_pass(parts):
    return pl.pallas_call(
        spread_kernel,
        out_shape=jax.ShapeDtypeStruct((16, 8, 128), jnp.float32),
        in_specs=[VMEM_SPEC],
        out_specs=VMEM_SPEC,
        compiler_params=SMALL,
        name="spread",
    )(parts)


def finish_kernel(parts_ref, weight_ref, key_ref, value_ref):
    total = jnp.sum(jnp.sum(parts_ref[...], axis=0))
    mean_square = total / (2.0 * MODEL_WIDTH * KEY_VALUE_HEADS * HEAD_SIZE)
    factor = 1.0 / jnp.sqrt(jnp.full((1, HEAD_SIZE), mean_square + 1e-06, jnp.float32))
    key_ref[...] = weight_ref[:, :HEAD_SIZE] * factor
    value_ref[...] = weight_ref[:, HEAD_SIZE:] * factor


def finish_pass(parts, weight):
    shape = jax.ShapeDtypeStruct((BLOCK_TOKENS, HEAD_SIZE), jnp.float32)
    return pl.pallas_call(
        finish_kernel,
        out_shape=(shape, shape),
        in_specs=[VMEM_SPEC, VMEM_SPEC],
        out_specs=(VMEM_SPEC, VMEM_SPEC),
        compiler_params=SMALL,
        name="finish",
    )(parts, weight)


def fan_kernel(src_ref, out_ref):
    out_ref[0] = src_ref[...]


def fan_out(tokens, copies):
    rows, width = tokens.shape
    return pl.pallas_call(
        fan_kernel,
        grid=(copies,),
        out_shape=jax.ShapeDtypeStruct((copies, rows, width), tokens.dtype),
        in_specs=[pl.BlockSpec((rows, width), lambda copy: (0, 0))],
        out_specs=pl.BlockSpec((1, rows, width), lambda copy: (copy, 0, 0)),
        compiler_params=SMALL,
        name="fan",
    )(tokens)


def rotary_tables(positions):
    half = HEAD_SIZE // 2
    freqs = 500000.0 ** (-(jnp.arange(half, dtype=jnp.float32) * 2.0) / HEAD_SIZE)
    angles = positions.astype(jnp.float32)[:, None] * freqs[None, :]
    cosine, sine = jnp.cos(angles), jnp.sin(angles)
    return jnp.concatenate([cosine, cosine], -1), jnp.concatenate([sine, sine], -1)


def exchange(value, axis):
    return lax.all_to_all(value, axis, split_axis=0, concat_axis=0, tiled=True)


def per_device(hidden, queries, keys, values, output_gradient, doc_blocks):
    z = lax.axis_index(Z)
    row = lax.axis_index("y")
    head = lax.axis_index("head")
    ends = jnp.cumsum(doc_blocks)
    blocks = SIDE * z + jnp.arange(SIDE)
    firsts = jnp.max(jnp.where(ends[None, :] <= blocks[:, None], ends[None, :], 0), axis=1)
    info = jnp.concatenate([jnp.stack([z, row]), firsts]).astype(jnp.int32)
    here = SIDE * z + row
    f32 = jnp.float32

    own = jnp.concatenate([keys, values], axis=1)[None]
    four = rotate(own, Z, 4)
    rows = jnp.stack([queries, output_gradient])
    query_rows = exchange(jnp.broadcast_to(rows, (SIDE,) + rows.shape), "y")
    even = jnp.concatenate([own, four])
    two = rotate(even, Z, 2)
    odd = rotate(jnp.concatenate([own, two[0:1], four]), Z, 1)
    column = jnp.concatenate([own, two[0:1], four, two[1:2], odd])

    picked, odd = lax.optimization_barrier((pick_features(hidden, head), odd))
    tokens = exchange(picked, "z_lo").reshape(SIDE * BLOCK_TOKENS, 256)
    stats = stats_pass(info, query_rows, column)
    tokens, stats = lax.optimization_barrier((tokens, stats))
    stats = exchange(stats, "y")
    tokens, stats = lax.optimization_barrier((fan_out(tokens, 8), stats))
    features = exchange(tokens, "head")
    odd_grads = grads_pass(ODD_GROUPS, jnp.bfloat16, info, query_rows, column, stats)
    odd_back = rotate(odd_grads, Z, -1)
    even_grads = grads_pass(EVEN_GROUPS, f32, info, query_rows, column, stats)
    odd_back = odd_back.astype(f32)
    s0 = even_grads[0] + odd_back[0]
    s2 = even_grads[1] + odd_back[1]
    s4 = even_grads[2] + odd_back[2]
    two_back = rotate(jnp.stack([s2, even_grads[3]]).astype(jnp.bfloat16), Z, -2).astype(f32)
    s0 = s0 + two_back[0]
    s4 = s4 + two_back[1]
    four_back = rotate(s4.astype(jnp.bfloat16), Z, -4)
    features, four_back = lax.optimization_barrier((features, four_back))
    s0 = s0 + four_back.astype(f32)

    cosine, sine = rotary_tables(here * BLOCK_TOKENS + jnp.arange(BLOCK_TOKENS))
    key_grad = s0[:, :HEAD_SIZE]
    half = HEAD_SIZE // 2
    turned = jnp.concatenate([-key_grad[:, half:], key_grad[:, :half]], axis=-1)
    pre = jnp.concatenate([key_grad * cosine - turned * sine, s0[:, HEAD_SIZE:]], axis=1)
    pre = pre.astype(jnp.bfloat16)
    gathered = exchange(jnp.broadcast_to(pre, (SIDE,) + pre.shape), "z_lo")
    gathered = gathered.reshape(SIDE * BLOCK_TOKENS, 2 * HEAD_SIZE)

    weight = lax.dot_general(
        features, gathered, (((1,), (0,)), ((), ())), preferred_element_type=f32
    ).astype(jnp.bfloat16)
    weight = exchange(weight.reshape(SIDE, SIDE * BLOCK_TOKENS, 256), "y")
    weight = jnp.sum(weight.astype(f32), axis=0).astype(jnp.bfloat16)
    weight = exchange(weight.reshape(SIDE, BLOCK_TOKENS, 256), "z_hi")
    weight, spread = square_pass(weight)
    spread = spread_pass(exchange(spread, ("y", "head")))
    return finish_pass(exchange(spread, Z), weight)


def solution(mesh):
    devices = mesh.devices.reshape(4, 4, 4, 8)
    split = Mesh(devices, ("z_hi", "z_lo", "y", "head"))
    placed = (P(CTX, None),) + (P(CTX, "head"),) * 4 + (P(),)
    return jax.shard_map(
        per_device,
        mesh=split,
        in_specs=placed,
        out_specs=(P(CTX, "head"), P(CTX, "head")),
        check_vma=False,
    )
```

```python
import functools

import jax
import jax.numpy as jnp
from jax import lax
from jax.experimental import pallas as pl
from jax.experimental.pallas import tpu as pltpu
from jax.sharding import Mesh, PartitionSpec as P

MODEL_WIDTH = 8192
QUERY_HEADS = 64
KEY_VALUE_HEADS = 8
HEAD_SIZE = 128
BLOCK_TOKENS = 128
GROUP = QUERY_HEADS // KEY_VALUE_HEADS
ROWS = GROUP * BLOCK_TOKENS
PLANES = 7
SIDE = 4
STATS = 2
ORDER = (0, 2, 4, 6, 1, 3, 5)
EVEN_GROUPS = ((0, 4),)
ODD_GROUPS = ((4, 7),)
NEGATIVE = -1e30
SCALE = HEAD_SIZE ** (-0.5)
LOG2E = 1.4426950408889634
EXP_SCALE = SCALE * LOG2E
Z = ("z_hi", "z_lo")
CTX = ("z_hi", "z_lo", "y")

NT = (((1,), (1,)), ((), ()))
NN = (((1,), (0,)), ((), ()))
TN = (((0,), (0,)), ((), ()))


def axis_total(axis):
    names = axis if isinstance(axis, tuple) else (axis,)
    total = 1
    for name in names:
        total *= lax.axis_size(name)
    return total


def rotate(value, axis, steps):
    count = axis_total(axis)
    return lax.ppermute(value, axis, [(at, (at + steps) % count) for at in range(count)])


def stack_heads(row_ref, which, dst_ref):
    for head in range(GROUP):
        dst_ref[head * BLOCK_TOKENS:(head + 1) * BLOCK_TOKENS, :] = row_ref[
            0, which, :, head * HEAD_SIZE:(head + 1) * HEAD_SIZE
        ]


def causal_mask(offset):
    token = lax.broadcasted_iota(jnp.int32, (BLOCK_TOKENS, ROWS), 0)
    query = lax.broadcasted_iota(jnp.int32, (BLOCK_TOKENS, ROWS), 1)
    return token <= (query & (BLOCK_TOKENS - 1)) + BLOCK_TOKENS * offset


def block_offset(info_ref, plane, query_row):
    offset = SIDE * plane + query_row - info_ref[1]
    position = SIDE * info_ref[0] + query_row
    return offset, (offset >= 0) & (position - offset >= info_ref[2 + query_row])


def group_valid(info_ref, first, last, query_row):
    return [block_offset(info_ref, ORDER[slot], query_row) for slot in range(first, last)]


def masked(value, checks, first, fill):
    parts = []
    for index, (offset, valid) in enumerate(checks):
        part = value[index * BLOCK_TOKENS:(index + 1) * BLOCK_TOKENS]
        keep = valid if ORDER[first + index] else valid & causal_mask(offset)
        parts.append(jnp.where(keep, part, fill))
    return parts[0] if len(parts) == 1 else jnp.concatenate(parts, axis=0)


def products(kv_ref, first, last, qs, gs):
    rows = (last - first) * BLOCK_TOKENS
    key = kv_ref[first:last, :, :HEAD_SIZE].reshape(rows, HEAD_SIZE)
    value = kv_ref[first:last, :, HEAD_SIZE:].reshape(rows, HEAD_SIZE)
    score = lax.dot_general(key, qs, NT, preferred_element_type=jnp.float32)
    dprob = lax.dot_general(value, gs, NT, preferred_element_type=jnp.float32)
    return score, dprob


def stats_kernel(info_ref, row_ref, kv_ref, out_ref, qs_ref, gs_ref, run_ref):
    query_row = pl.program_id(0)
    stack_heads(row_ref, 0, qs_ref)
    stack_heads(row_ref, 1, gs_ref)
    run_ref[0:1, :] = jnp.full((1, ROWS), NEGATIVE, jnp.float32)
    run_ref[1:, :] = jnp.zeros((7, ROWS), jnp.float32)
    for first, last in EVEN_GROUPS + ODD_GROUPS:
        checks = group_valid(info_ref, first, last, query_row)

        @pl.when(functools.reduce(jnp.logical_or, [valid for _, valid in checks]))
        def _():
            score, dprob = products(kv_ref, first, last, qs_ref[...], gs_ref[...])
            score = masked(score, checks, first, NEGATIVE)
            old = run_ref[0:1, :]
            top = jnp.maximum(old, jnp.max(score, axis=0, keepdims=True))
            weight = jnp.exp2((score - top) * EXP_SCALE)
            keep = jnp.exp2((old - top) * EXP_SCALE)
            run_ref[0:1, :] = top
            run_ref[1:2, :] = run_ref[1:2, :] * keep + jnp.sum(weight, axis=0, keepdims=True)
            run_ref[2:3, :] = run_ref[2:3, :] * keep + jnp.sum(
                weight * dprob, axis=0, keepdims=True
            )

    total = run_ref[1:2, :]
    some = total > 0.0
    safe = jnp.where(some, total, 1.0)
    lse = jnp.where(some, run_ref[0:1, :] * EXP_SCALE + jnp.log2(safe), NEGATIVE)
    mean = run_ref[2:3, :] / safe
    for target in range(SIDE):
        out_ref[target, 0, 0:1, :] = lse
        out_ref[target, 0, 1:2, :] = mean


def grads_kernel(groups, info_ref, row_ref, kv_ref, stats_ref, out_ref, qs_ref, gs_ref, acc_ref):
    query_row = pl.program_id(0)
    base = groups[0][0]

    @pl.when(query_row == 0)
    def _():
        acc_ref[...] = jnp.zeros(acc_ref.shape, jnp.float32)

    stack_heads(row_ref, 0, qs_ref)
    stack_heads(row_ref, 1, gs_ref)
    parts = [stats_ref[source, 0, 0:1, :] for source in range(SIDE)]
    top = functools.reduce(jnp.maximum, parts)
    shares = [jnp.exp2(part - top) for part in parts]
    total = sum(shares)
    lse = top + jnp.log2(total)
    inner = sum(stats_ref[source, 0, 1:2, :] * shares[source] for source in range(SIDE))
    delta = inner / total
    for first, last in groups:
        checks = group_valid(info_ref, first, last, query_row)

        @pl.when(functools.reduce(jnp.logical_or, [valid for _, valid in checks]))
        def _():
            qs, gs = qs_ref[...], gs_ref[...]
            score, dprob = products(kv_ref, first, last, qs, gs)
            prob = masked(jnp.exp2(score * EXP_SCALE - lse), checks, first, 0.0)
            dscore = (prob * (dprob - delta)).astype(jnp.bfloat16)
            key_part = lax.dot_general(dscore, qs, NN, preferred_element_type=jnp.float32)
            value_part = lax.dot_general(
                prob.astype(jnp.bfloat16), gs, NN, preferred_element_type=jnp.float32
            )
            shape = (last - first, BLOCK_TOKENS, HEAD_SIZE)
            at = slice(first - base, last - base)
            acc_ref[at, :, :HEAD_SIZE] += (key_part * SCALE).reshape(shape)
            acc_ref[at, :, HEAD_SIZE:] += value_part.reshape(shape)

    @pl.when(query_row == SIDE - 1)
    def _():
        out_ref[...] = acc_ref[...].astype(out_ref.dtype)


STACKS = [
    pltpu.VMEM((ROWS, HEAD_SIZE), jnp.bfloat16),
    pltpu.VMEM((ROWS, HEAD_SIZE), jnp.bfloat16),
]
PARAMS = pltpu.CompilerParams(vmem_limit_bytes=40 * 1024 * 1024)
SMALL = pltpu.CompilerParams(vmem_limit_bytes=8 * 1024 * 1024)
ROW_SHAPE = (1, 2, BLOCK_TOKENS, GROUP * HEAD_SIZE)
ROW_SPEC = pl.BlockSpec(ROW_SHAPE, lambda step, info: (step, 0, 0, 0))
STATS_SPEC = pl.BlockSpec((SIDE, 1, STATS, ROWS), lambda step, info: (0, step, 0, 0))


def whole(shape):
    return pl.BlockSpec(shape, lambda step, info: (0,) * len(shape))


def stats_pass(info, rows, kv):
    spec = pltpu.PrefetchScalarGridSpec(
        num_scalar_prefetch=1,
        grid=(SIDE,),
        in_specs=[ROW_SPEC, whole(kv.shape)],
        out_specs=STATS_SPEC,
        scratch_shapes=STACKS + [pltpu.VMEM((8, ROWS), jnp.float32)],
    )
    return pl.pallas_call(
        stats_kernel,
        out_shape=jax.ShapeDtypeStruct((SIDE, SIDE, STATS, ROWS), jnp.float32),
        grid_spec=spec,
        compiler_params=PARAMS,
        name="stats",
    )(info, rows, kv)


def grads_pass(groups, dtype, info, rows, kv, stats):
    shape = (groups[-1][1] - groups[0][0], BLOCK_TOKENS, 2 * HEAD_SIZE)
    spec = pltpu.PrefetchScalarGridSpec(
        num_scalar_prefetch=1,
        grid=(SIDE,),
        in_specs=[ROW_SPEC, whole(kv.shape), STATS_SPEC],
        out_specs=whole(shape),
        scratch_shapes=STACKS + [pltpu.VMEM(shape, jnp.float32)],
    )
    return pl.pallas_call(
        functools.partial(grads_kernel, groups),
        out_shape=jax.ShapeDtypeStruct(shape, dtype),
        grid_spec=spec,
        compiler_params=PARAMS,
        name="grads" + str(groups[0][0]),
    )(info, rows, kv, stats)


def pick_kernel(pick_ref, left_ref, right_ref, out_ref):
    out_ref[0, :, :128] = left_ref[...]
    out_ref[0, :, 128:] = right_ref[...]


def pick_features(hidden, head):
    pick = jnp.stack([2 * (head % 2), head // 2]).astype(jnp.int32)

    def half_spec(half):
        return pl.BlockSpec(
            (BLOCK_TOKENS, 128), lambda lo, pick: (0, (pick[0] + half) * 16 + lo * 4 + pick[1])
        )

    spec = pltpu.PrefetchScalarGridSpec(
        num_scalar_prefetch=1,
        grid=(SIDE,),
        in_specs=[half_spec(0), half_spec(1)],
        out_specs=pl.BlockSpec((1, BLOCK_TOKENS, 256), lambda lo, pick: (lo, 0, 0)),
    )
    return pl.pallas_call(
        pick_kernel,
        out_shape=jax.ShapeDtypeStruct((SIDE, BLOCK_TOKENS, 256), hidden.dtype),
        grid_spec=spec,
        compiler_params=SMALL,
        name="pick",
    )(pick, hidden, hidden)


VMEM_SPEC = pl.BlockSpec(memory_space=pltpu.VMEM)


def square_kernel(parts_ref, weight_ref, spread_ref):
    weight = sum(parts_ref[source].astype(jnp.float32) for source in range(SIDE))
    weight_ref[...] = weight
    squares = jnp.sum((weight * weight).reshape(16, 8, 256), axis=0)
    squares = squares[:, :128] + squares[:, 128:]
    spread_ref[...] = jnp.broadcast_to(squares, spread_ref.shape)


def square_pass(parts):
    return pl.pallas_call(
        square_kernel,
        out_shape=(
            jax.ShapeDtypeStruct((BLOCK_TOKENS, 256), jnp.float32),
            jax.ShapeDtypeStruct((32, 8, 128), jnp.float32),
        ),
        in_specs=[VMEM_SPEC],
        out_specs=(VMEM_SPEC, VMEM_SPEC),
        compiler_params=SMALL,
        name="square",
    )(parts)


def spread_kernel(parts_ref, out_ref):
    out_ref[...] = jnp.broadcast_to(jnp.sum(parts_ref[...], axis=0), out_ref.shape)


def spread_pass(parts):
    return pl.pallas_call(
        spread_kernel,
        out_shape=jax.ShapeDtypeStruct((16, 8, 128), jnp.float32),
        in_specs=[VMEM_SPEC],
        out_specs=VMEM_SPEC,
        compiler_params=SMALL,
        name="spread",
    )(parts)


def finish_kernel(parts_ref, weight_ref, key_ref, value_ref):
    total = jnp.sum(jnp.sum(parts_ref[...], axis=0))
    mean_square = total / (2.0 * MODEL_WIDTH * KEY_VALUE_HEADS * HEAD_SIZE)
    factor = 1.0 / jnp.sqrt(jnp.full((1, HEAD_SIZE), mean_square + 1e-06, jnp.float32))
    key_ref[...] = weight_ref[:, :HEAD_SIZE] * factor
    value_ref[...] = weight_ref[:, HEAD_SIZE:] * factor


def finish_pass(parts, weight):
    shape = jax.ShapeDtypeStruct((BLOCK_TOKENS, HEAD_SIZE), jnp.float32)
    return pl.pallas_call(
        finish_kernel,
        out_shape=(shape, shape),
        in_specs=[VMEM_SPEC, VMEM_SPEC],
        out_specs=(VMEM_SPEC, VMEM_SPEC),
        compiler_params=SMALL,
        name="finish",
    )(parts, weight)


def fan_kernel(src_ref, out_ref):
    out_ref[0] = src_ref[...]


def fan_out(tokens, copies):
    rows, width = tokens.shape
    return pl.pallas_call(
        fan_kernel,
        grid=(copies,),
        out_shape=jax.ShapeDtypeStruct((copies, rows, width), tokens.dtype),
        in_specs=[pl.BlockSpec((rows, width), lambda copy: (0, 0))],
        out_specs=pl.BlockSpec((1, rows, width), lambda copy: (copy, 0, 0)),
        compiler_params=SMALL,
        name="fan",
    )(tokens)


def pair_kernel(q_ref, g_ref, out_ref):
    out_ref[0, 0] = q_ref[...]
    out_ref[0, 1] = g_ref[...]


def pair_out(queries, gradients):
    shape = queries.shape
    return pl.pallas_call(
        pair_kernel,
        grid=(SIDE,),
        out_shape=jax.ShapeDtypeStruct((SIDE, 2) + shape, queries.dtype),
        in_specs=[pl.BlockSpec(shape, lambda copy: (0, 0))] * 2,
        out_specs=pl.BlockSpec((1, 2) + shape, lambda copy: (copy, 0, 0, 0)),
        compiler_params=SMALL,
        name="pair",
    )(queries, gradients)


def rotary_tables(positions):
    half = HEAD_SIZE // 2
    freqs = 500000.0 ** (-(jnp.arange(half, dtype=jnp.float32) * 2.0) / HEAD_SIZE)
    angles = positions.astype(jnp.float32)[:, None] * freqs[None, :]
    cosine, sine = jnp.cos(angles), jnp.sin(angles)
    return jnp.concatenate([cosine, cosine], -1), jnp.concatenate([sine, sine], -1)


def exchange(value, axis):
    return lax.all_to_all(value, axis, split_axis=0, concat_axis=0, tiled=True)


def per_device(hidden, queries, keys, values, output_gradient, doc_blocks):
    z = lax.axis_index(Z)
    row = lax.axis_index("y")
    head = lax.axis_index("head")
    ends = jnp.cumsum(doc_blocks)
    blocks = SIDE * z + jnp.arange(SIDE)
    firsts = jnp.max(jnp.where(ends[None, :] <= blocks[:, None], ends[None, :], 0), axis=1)
    info = jnp.concatenate([jnp.stack([z, row]), firsts]).astype(jnp.int32)
    here = SIDE * z + row
    f32 = jnp.float32

    own = jnp.concatenate([keys, values], axis=1)[None]
    four = rotate(own, Z, 4)
    query_rows = exchange(pair_out(queries, output_gradient), "y")
    even = jnp.concatenate([own, four])
    two = rotate(even, Z, 2)
    odd = rotate(jnp.concatenate([own, two[0:1], four]), Z, 1)
    column = jnp.concatenate([own, two[0:1], four, two[1:2], odd])

    picked, odd = lax.optimization_barrier((pick_features(hidden, head), odd))
    tokens = exchange(picked, "z_lo").reshape(SIDE * BLOCK_TOKENS, 256)
    stats = stats_pass(info, query_rows, column)
    tokens, stats = lax.optimization_barrier((tokens, stats))
    stats = exchange(stats, "y")
    tokens, stats = lax.optimization_barrier((fan_out(tokens, 8), stats))
    features = exchange(tokens, "head")
    odd_grads = grads_pass(ODD_GROUPS, jnp.bfloat16, info, query_rows, column, stats)
    odd_back = rotate(odd_grads, Z, -1)
    even_grads = grads_pass(EVEN_GROUPS, f32, info, query_rows, column, stats)
    odd_back = odd_back.astype(f32)
    s0 = even_grads[0] + odd_back[0]
    s2 = even_grads[1] + odd_back[1]
    s4 = even_grads[2] + odd_back[2]
    two_back = rotate(jnp.stack([s2, even_grads[3]]).astype(jnp.bfloat16), Z, -2).astype(f32)
    s0 = s0 + two_back[0]
    s4 = s4 + two_back[1]
    four_back = rotate(s4.astype(jnp.bfloat16), Z, -4)
    features, four_back = lax.optimization_barrier((features, four_back))
    s0 = s0 + four_back.astype(f32)

    cosine, sine = rotary_tables(here * BLOCK_TOKENS + jnp.arange(BLOCK_TOKENS))
    key_grad = s0[:, :HEAD_SIZE]
    half = HEAD_SIZE // 2
    turned = jnp.concatenate([-key_grad[:, half:], key_grad[:, :half]], axis=-1)
    pre = jnp.concatenate([key_grad * cosine - turned * sine, s0[:, HEAD_SIZE:]], axis=1)
    pre = pre.astype(jnp.bfloat16)
    gathered = exchange(jnp.broadcast_to(pre, (SIDE,) + pre.shape), "z_lo")
    gathered = gathered.reshape(SIDE * BLOCK_TOKENS, 2 * HEAD_SIZE)

    weight = lax.dot_general(
        features, gathered, (((1,), (0,)), ((), ())), preferred_element_type=f32
    ).astype(jnp.bfloat16)
    weight = exchange(weight.reshape(SIDE, SIDE * BLOCK_TOKENS, 256), "y")
    weight = jnp.sum(weight.astype(f32), axis=0).astype(jnp.bfloat16)
    weight = exchange(weight.reshape(SIDE, BLOCK_TOKENS, 256), "z_hi")
    weight, spread = square_pass(weight)
    spread = spread_pass(exchange(spread, ("y", "head")))
    return finish_pass(exchange(spread, Z), weight)


def solution(mesh):
    devices = mesh.devices.reshape(4, 4, 4, 8)
    split = Mesh(devices, ("z_hi", "z_lo", "y", "head"))
    placed = (P(CTX, None),) + (P(CTX, "head"),) * 4 + (P(),)
    return jax.shard_map(
        per_device,
        mesh=split,
        in_specs=placed,
        out_specs=(P(CTX, "head"), P(CTX, "head")),
        check_vma=False,
    )
```
